32 devices in a mesh: groups: 2 (over y), rows: 4 (over z), cols: 4 (over x, core).
Axes of the slice: x: 2, y: 2, z: 4, core: 2. Of those that a mesh axis runs over, the one named last changes fastest.
Arguments:
- query_grid: bfloat16 [128, 96, 768], P(('groups', 'rows'), 'cols'), parts along dimension 0, may hold values from -9 to 9
- key_grid: bfloat16 [128, 96, 768], P(('groups', 'rows'), 'cols'), parts along dimension 0, may hold values from -9 to 9
- value_grid: bfloat16 [128, 96, 768], P(('groups', 'rows'), 'cols'), parts along dimension 0, may hold values from -6 to 6
- out_grad: bfloat16 [128, 96, 768], P(('groups', 'rows'), 'cols'), parts along dimension 0, may hold values from -6 to 6
- tissue: int32 [16, 12], P(('groups', 'rows'), 'cols'), parts along dimension 0, may hold values from 0 to 1, as said below
Outputs:
- attended: bfloat16 [128, 96, 768], P(('groups', 'rows'), 'cols'), parts along dimension 0
- grad_query: bfloat16 [128, 96, 768], P(('groups', 'rows'), 'cols'), parts along dimension 0
- grad_key: bfloat16 [128, 96, 768], P(('groups', 'rows'), 'cols'), parts along dimension 0
- grad_value: bfloat16 [128, 96, 768], P(('groups', 'rows'), 'cols'), parts along dimension 0
The draws below stay inside these ranges and needn't reach their ends.
There are 2 independent parts, one for each index of `groups`. The reference program is written for one: setup_inputs(seed, part) draws one part's arguments, and reference() takes and returns one part's arrays. A program takes and returns all parts, laid end to end along the dimension named above; each array names one. Nothing has to cross between parts.
Inputs may be any that keep to these rules, and one draw needn't show every extreme that they name: 1 marks a tile of tissue.
All inputs are finite; a program needn't handle non-finite values.
Results may differ from the reference program's by a relative error of at most 0.019.
Values may be sent and summed in bfloat16 or wider, within the bound.
No kernel may reach another device: no remote copies, remote signals or barrier semaphores. Data moves between devices by JAX's collectives and lax.ppermute only.
A program may use at most 128 MiB of HBM per device.

```python
import jax
import jax.numpy as jnp
from jax import lax

D = 768
HEADS = 12
HEAD = 64
TILE = 8
TILES_R = 8
TILES_C = 12
GRID_R = 64
GRID_C = 96


def draw_pair(key):
    base_key = jax.random.fold_in(key, 7)
    query_key, key_key = jax.random.split(base_key, 2)
    grid_shape = (GRID_R, GRID_C, D)
    query_base = jnp.clip(jax.random.normal(query_key, grid_shape, jnp.float32), -6.0, 6.0)
    key_base = jnp.clip(jax.random.normal(key_key, grid_shape, jnp.float32), -6.0, 6.0)
    return (query_base, key_base)


def draw_query_grid(key, part):
    return draw_pair(key)[0].astype(jnp.bfloat16)


def draw_key_grid(key, part):
    return draw_pair(key)[1].astype(jnp.bfloat16)


def draw_tissue(key, part):
    keys_all = jax.random.split(jax.random.fold_in(key, 11), 6)
    centre_row = jax.random.randint(keys_all[0], (), 0, TILES_R)
    centre_col = jax.random.randint(keys_all[1], (), 0, TILES_C)
    radius_row = jax.random.randint(keys_all[2], (), TILES_R // 4 + 1, TILES_R // 2 + 2)
    radius_col = jax.random.randint(keys_all[3], (), TILES_C // 4 + 1, TILES_C // 2 + 2)
    row_off = jnp.arange(TILES_R, dtype=jnp.int32)[:, None] - centre_row
    col_off = jnp.arange(TILES_C, dtype=jnp.int32)[None, :] - centre_col
    inside = row_off * row_off * radius_col * radius_col + col_off * col_off * radius_row * radius_row <= radius_row * radius_row * radius_col * radius_col
    holes = jax.random.randint(keys_all[4], (TILES_R, TILES_C), 0, 6) == 0
    strays = jax.random.randint(keys_all[5], (TILES_R, TILES_C), 0, 8) == 0
    return jnp.where(inside, jnp.logical_not(holes), strays).astype(jnp.int32)


def shard_levels(rng, shape, cuts, smallest, top_value):
    def one(position, shards_of):
        steps = jax.random.uniform(jax.random.fold_in(jax.random.fold_in(rng, 6), position), (shards_of,), jnp.float32, smallest / len(cuts), top_value / len(cuts))
        return jnp.repeat(jnp.exp(steps), shape[position] // shards_of).reshape((-1,) + (1,) * (len(shape) - position - 1))

    factor_of = one(*cuts[0])
    for cut in cuts[1:]:
        factor_of = factor_of * one(*cut)
    return factor_of


def noise(own_key, shape, width, most, cuts=(), held_as=jnp.bfloat16):
    factor_of = shard_levels(own_key, shape, cuts, -0.22, 0.18) if cuts else 1.0
    drawn = jax.random.normal(own_key, shape, jnp.float32) * width * factor_of
    return jnp.minimum(jnp.maximum(drawn, -most), most).astype(held_as)


def setup_inputs(seed: int = 0, part: int = 0) -> dict:
    arg_keys = jax.random.split(jax.random.key(seed), 6)
    own_keys = jax.random.split(jax.random.fold_in(arg_keys[5], part), 6)
    return {
        "query_grid": draw_query_grid(jax.random.fold_in(jax.random.fold_in(arg_keys[5], part), 71), part),
        "key_grid": draw_key_grid(jax.random.fold_in(jax.random.fold_in(arg_keys[5], part), 71), part),
        "value_grid": noise(own_keys[2], (GRID_R, GRID_C, D), 1.0, 6.0, ((0, 4), (1, 4))),
        "out_grad": noise(own_keys[3], (GRID_R, GRID_C, D), 1.0, 6.0, ((0, 4), (1, 4))),
        "tissue": draw_tissue(jax.random.fold_in(jax.random.fold_in(arg_keys[5], part), 71), part),
    }


NEG = -1.0e30


def trailing(first, array):
    return tuple(range(first, array.ndim))


def row_tiles(stripe, number):
    inner_shape = stripe.shape[2:]
    shaped = stripe.reshape((TILE, number, TILE) + inner_shape)
    return shaped.transpose((1, 0, 2) + trailing(3, shaped)).reshape((number, TILE * TILE) + inner_shape)


def tiles_rows(tiles, number):
    inner_shape = tiles.shape[2:]
    shaped = tiles.reshape((number, TILE, TILE) + inner_shape)
    return shaped.transpose((1, 0, 2) + trailing(3, shaped)).reshape((TILE, number * TILE) + inner_shape)


def neighbour_tiles(stripe, number):
    inner_shape = stripe.shape[2:]
    shaped = stripe.reshape((3, TILE, number + 2, TILE) + inner_shape)
    pieces = jnp.stack([shaped[:, :, column:column + number] for column in range(3)], axis=0)
    reordered = pieces.transpose((3, 1, 0, 2, 4) + trailing(5, pieces))
    return reordered.reshape((number, 9 * TILE * TILE) + inner_shape)


def neighbour_marks(stripe, number):
    pieces = jnp.stack([stripe[:, column:column + number] for column in range(3)], axis=0)
    reordered = pieces.transpose(2, 1, 0).reshape(number, 9, 1)
    return jnp.broadcast_to(reordered, (number, 9, TILE * TILE)).reshape(number, 9 * TILE * TILE)


def pair_allowed(own_marks, near_marks):
    own_tile = (jnp.arange(9 * TILE * TILE, dtype=jnp.int32) // (TILE * TILE)) == 4
    return jnp.logical_or(own_marks[:, None] * near_marks > 0, own_tile[None, :])


def split_heads(tiles):
    return tiles.reshape(tiles.shape[:2] + (HEADS, HEAD))


def query_pass(query_tiles, grad_tiles, key_tiles, value_tiles, query_marks, key_marks):
    score_scale = HEAD ** -0.5
    number = query_tiles.shape[0]
    query_heads = split_heads(query_tiles).astype(jnp.float32)
    key_heads = split_heads(key_tiles).astype(jnp.float32)
    value_heads = split_heads(value_tiles).astype(jnp.float32)
    grad_heads = split_heads(grad_tiles).astype(jnp.float32)
    allowed = pair_allowed(query_marks, key_marks)[:, None, None, :]
    scores = jnp.einsum("tqhd,tkhd->thqk", query_heads, key_heads) * score_scale
    masked = jnp.where(allowed, scores, NEG)
    row_max = jnp.max(masked, axis=-1, keepdims=True)
    row_sum = jnp.sum(jnp.where(allowed, jnp.exp(masked - row_max), 0.0), axis=-1, keepdims=True)
    log_total = row_max + jnp.log(row_sum)
    attn_probs = jnp.where(allowed, jnp.exp(masked - log_total), 0.0)
    probs_low = lax.optimization_barrier(attn_probs.astype(jnp.bfloat16)).astype(jnp.float32)
    query_mark = query_marks.astype(jnp.float32)[:, None, None, None]
    attended = jnp.einsum("thqk,tkhd->tqhd", probs_low, value_heads) * query_mark
    attended_low = lax.optimization_barrier(attended.astype(jnp.bfloat16))
    row_dot = jnp.sum(grad_heads * attended_low.astype(jnp.float32), axis=-1).transpose(0, 2, 1)[..., None]
    grad_probs = jnp.einsum("tqhd,tkhd->thqk", grad_heads, value_heads)
    grad_scores = (attn_probs * (grad_probs - row_dot) * score_scale).astype(jnp.bfloat16)
    grad_scores = lax.optimization_barrier(grad_scores).astype(jnp.float32)
    grad_query = jnp.einsum("thqk,tkhd->tqhd", grad_scores, key_heads).astype(jnp.bfloat16)
    return (attended_low.reshape(number, TILE * TILE, D), grad_query.reshape(number, TILE * TILE, D),
            log_total[..., 0], row_dot[..., 0])


def key_pass(key_tiles, value_tiles, query_tiles, grad_tiles, log_total, row_dot, key_marks, query_marks):
    score_scale = HEAD ** -0.5
    number = key_tiles.shape[0]
    query_heads = split_heads(query_tiles).astype(jnp.float32)
    key_heads = split_heads(key_tiles).astype(jnp.float32)
    value_heads = split_heads(value_tiles).astype(jnp.float32)
    grad_heads = split_heads(grad_tiles).astype(jnp.float32)
    allowed = pair_allowed(key_marks, query_marks)[:, None, :, None]
    scores = jnp.einsum("tqhd,tkhd->thqk", query_heads, key_heads) * score_scale
    attn_probs = jnp.where(allowed, jnp.exp(jnp.where(allowed, scores, NEG) - log_total[..., None]), 0.0)
    probs_low = lax.optimization_barrier(attn_probs.astype(jnp.bfloat16)).astype(jnp.float32)
    grad_value = jnp.einsum("thqk,tqhd->tkhd", probs_low, grad_heads).astype(jnp.bfloat16)
    grad_probs = jnp.einsum("tqhd,tkhd->thqk", grad_heads, value_heads)
    grad_scores = (attn_probs * (grad_probs - row_dot[..., None]) * score_scale).astype(jnp.bfloat16)
    grad_scores = lax.optimization_barrier(grad_scores).astype(jnp.float32)
    grad_key = jnp.einsum("thqk,tqhd->tkhd", grad_scores, query_heads).astype(jnp.bfloat16)
    return grad_key.reshape(number, TILE * TILE, D), grad_value.reshape(number, TILE * TILE, D)


def reference(query_grid, key_grid, value_grid, out_grad, tissue):
    expand = jnp.broadcast_to(tissue[:, None, :, None], (TILES_R, TILE, TILES_C, TILE)).reshape(GRID_R, GRID_C)
    masked_grad = out_grad * expand.astype(jnp.bfloat16)[..., None]
    widths = ((TILE, TILE), (TILE, TILE), (0, 0), (0, 0))
    pair_pad = jnp.pad(jnp.stack((key_grid, value_grid), axis=2), widths)
    marks_pad = jnp.pad(tissue, 1)

    def first_pass(row_index):
        first_row = row_index * TILE
        near_pairs = neighbour_tiles(lax.dynamic_slice_in_dim(pair_pad, first_row, 3 * TILE, 0), TILES_C)
        key_marks = neighbour_marks(lax.dynamic_slice_in_dim(marks_pad, row_index, 3, 0), TILES_C)
        query_marks = lax.dynamic_slice_in_dim(tissue, row_index, 1, 0)[0]
        query_tiles = row_tiles(lax.dynamic_slice_in_dim(query_grid, first_row, TILE, 0), TILES_C)
        grad_tiles = row_tiles(lax.dynamic_slice_in_dim(masked_grad, first_row, TILE, 0), TILES_C)
        attended, grad_query, log_total, row_dot = query_pass(
            query_tiles, grad_tiles, near_pairs[:, :, 0], near_pairs[:, :, 1], query_marks, key_marks)
        row_stats = jnp.stack((log_total, row_dot), axis=-1).transpose(0, 2, 3, 1)
        return tiles_rows(attended, TILES_C), tiles_rows(grad_query, TILES_C), tiles_rows(row_stats, TILES_C)

    attended, grad_query, row_stats = lax.map(first_pass, jnp.arange(TILES_R, dtype=jnp.int32))
    attended = attended.reshape(GRID_R, GRID_C, D)
    grad_query = grad_query.reshape(GRID_R, GRID_C, D)
    row_stats = row_stats.reshape(GRID_R, GRID_C, 2, HEADS)
    query_pad = jnp.pad(jnp.stack((query_grid, masked_grad), axis=2), widths)
    stats_pad = jnp.pad(row_stats, widths)

    def second_pass(row_index):
        first_row = row_index * TILE
        near_pairs = neighbour_tiles(lax.dynamic_slice_in_dim(query_pad, first_row, 3 * TILE, 0), TILES_C)
        near_stats = neighbour_tiles(lax.dynamic_slice_in_dim(stats_pad, first_row, 3 * TILE, 0), TILES_C)
        query_marks = neighbour_marks(lax.dynamic_slice_in_dim(marks_pad, row_index, 3, 0), TILES_C)
        key_marks = lax.dynamic_slice_in_dim(tissue, row_index, 1, 0)[0]
        key_tiles = row_tiles(lax.dynamic_slice_in_dim(key_grid, first_row, TILE, 0), TILES_C)
        value_tiles = row_tiles(lax.dynamic_slice_in_dim(value_grid, first_row, TILE, 0), TILES_C)
        log_total = near_stats[:, :, 0].transpose(0, 2, 1)
        row_dot = near_stats[:, :, 1].transpose(0, 2, 1)
        grad_key, grad_value = key_pass(key_tiles, value_tiles, near_pairs[:, :, 0], near_pairs[:, :, 1],
                                        log_total, row_dot, key_marks, query_marks)
        return tiles_rows(grad_key, TILES_C), tiles_rows(grad_value, TILES_C)

    grad_key, grad_value = lax.map(second_pass, jnp.arange(TILES_R, dtype=jnp.int32))
    return (attended, grad_query, grad_key.reshape(GRID_R, GRID_C, D), grad_value.reshape(GRID_R, GRID_C, D))
```

```python
import jax
import jax.numpy as jnp
from jax import lax
from jax.experimental import pallas as pl
from jax.experimental.pallas import tpu as pltpu
from jax.sharding import PartitionSpec as P

HEAD = 64
TILE = 8
TOKENS = TILE * TILE
LANES = 256
PER = LANES // HEAD
SCALE = HEAD ** -0.5
LOG2E = 1.4426950408889634
NEG = -1e30
BIG = 1e30
LIMIT = 56 * 1024 * 1024


def shift(array, axis, by):
    count = lax.axis_size(axis)
    pairs = [(i, i + by) for i in range(count) if 0 <= i + by < count]
    return lax.ppermute(array, axis, pairs)


def nt(a, b):
    return lax.dot_general(a, b, (((1,), (1,)), ((), ())), preferred_element_type=jnp.float32)


def nn(a, b):
    return lax.dot_general(a, b, (((1,), (0,)), ((), ())), preferred_element_type=jnp.float32)


def tn(a, b):
    return lax.dot_general(a, b, (((0,), (0,)), ((), ())), preferred_element_type=jnp.float32)


def tile_of(ref, a, b):
    block = ref[TILE * a : TILE * (a + 1), TILE * b : TILE * (b + 1), :]
    return block.astype(jnp.float32).reshape(TOKENS, block.shape[-1])


def put_tile(ref, a, b, value):
    shaped = value.reshape(TILE, TILE, value.shape[-1]).astype(ref.dtype)
    ref[TILE * a : TILE * (a + 1), TILE * b : TILE * (b + 1), :] = shaped


def pack(first, second, tissue, scaled):
    rows, cols = tissue.shape
    width = first.shape[-1]

    def body(mark_ref, first_ref, second_ref, *outs):
        row_refs, left_ref, right_ref = outs[:rows], outs[rows], outs[rows + 1]
        for a in range(rows):
            for b in range(cols):
                for n, ref in enumerate((first_ref, second_ref)):
                    tile = tile_of(ref, a, b)
                    if scaled:
                        tile = tile * (SCALE if n == 0 else mark_ref[a, b].astype(jnp.float32))
                    tile = tile.astype(jnp.bfloat16)
                    row_refs[a][n, b] = tile
                    if b == 0:
                        left_ref[n, a] = tile
                    if b == cols - 1:
                        right_ref[n, a] = tile

    row_shape = jax.ShapeDtypeStruct((2, cols, TOKENS, width), jnp.bfloat16)
    side_shape = jax.ShapeDtypeStruct((2, rows, TOKENS, width), jnp.bfloat16)
    vmem = pl.BlockSpec(memory_space=pltpu.VMEM)
    return pl.pallas_call(
        body,
        in_specs=[pl.BlockSpec(memory_space=pltpu.SMEM), vmem, vmem],
        out_specs=[vmem] * (rows + 2),
        out_shape=[row_shape] * rows + [side_shape] * 2,
        compiler_params=pltpu.CompilerParams(vmem_limit_bytes=LIMIT),
    )(tissue, first, second)


def halo(row_first, row_last, left, right):
    above = shift(row_last, "rows", 1)
    below = shift(row_first, "rows", -1)
    from_left = shift(right, "cols", 1)
    from_right = shift(left, "cols", -1)
    corner_left = shift(jnp.stack((above[:, -1], below[:, -1]), axis=1), "cols", 1)
    corner_right = shift(jnp.stack((above[:, 0], below[:, 0]), axis=1), "cols", -1)
    return above, below, from_left, from_right, corner_left, corner_right


def head_mask():
    row = lax.broadcasted_iota(jnp.int32, (LANES, LANES), 0) // HEAD
    lane = lax.broadcasted_iota(jnp.int32, (LANES, LANES), 1) // HEAD
    return row == lane


def spread(tile, mask):
    return jnp.where(mask, jnp.concatenate([tile] * PER, axis=0), jnp.zeros((), tile.dtype))


def gather_heads(full):
    lane = lax.broadcasted_iota(jnp.int32, (TOKENS, LANES), 1) // HEAD
    out = full[:TOKENS]
    for h in range(1, PER):
        out = jnp.where(lane == h, full[h * TOKENS : (h + 1) * TOKENS], out)
    return out


class Ext:
    def __init__(self, rows, cols, own, near):
        self.rows, self.cols, self.own, self.near = rows, cols, own, near

    def at(self, n, i, j):
        above, below, left, right, corner_left, corner_right = self.near
        if 0 <= i < self.rows:
            if j < 0:
                return left[n, i]
            if j >= self.cols:
                return right[n, i]
            return self.own[i][n, j]
        end = 0 if i < 0 else 1
        if j < 0:
            return corner_left[n, end]
        if j >= self.cols:
            return corner_right[n, end]
        return (above, below)[end][n, j]


def query_kernel(rows, cols):
    def body(mark_ref, *refs):
        own_kv, refs = refs[:rows], refs[rows:]
        near_kv, refs = refs[:6], refs[6:]
        own_qg, refs = refs[:rows], refs[rows:]
        att_ref, gq_ref, stat_refs = refs[0], refs[1], refs[2 : 2 + rows]
        sum_ref, s_ref, e_ref = refs[2 + rows :]
        keys = Ext(rows, cols, own_kv, near_kv)
        mask = head_mask()
        sum_ref[...] = jnp.zeros(sum_ref.shape, jnp.float32)
        for a in range(rows):
            for b in range(cols):
                places = [(a + i, b + j) for i in (-1, 0, 1) for j in (-1, 0, 1)]
                own_mark = mark_ref[a + 1, b + 1]
                allowed = [
                    True if (i, j) == (a, b) else own_mark * mark_ref[i + 1, j + 1] > 0
                    for i, j in places
                ]
                q = spread(own_qg[a][0, b], mask)
                g = spread(own_qg[a][1, b], mask)
                top = jnp.full((1, LANES), NEG, jnp.float32)
                for t, (i, j) in enumerate(places):
                    s = nt(keys.at(0, i, j), q)
                    s_ref[t * TOKENS : (t + 1) * TOKENS] = s
                    high = jnp.max(s, axis=0, keepdims=True)
                    top = jnp.maximum(top, jnp.where(allowed[t], high, NEG))
                top = top * LOG2E
                total = jnp.zeros((1, LANES), jnp.float32)
                for t in range(9):
                    e = jnp.exp2(s_ref[t * TOKENS : (t + 1) * TOKENS] * LOG2E - jnp.where(allowed[t], top, BIG))
                    s_ref[t * TOKENS : (t + 1) * TOKENS] = e
                    total = total + jnp.sum(e, axis=0, keepdims=True)
                inv = 1.0 / total
                for t in range(9):
                    p = s_ref[t * TOKENS : (t + 1) * TOKENS] * inv
                    s_ref[t * TOKENS : (t + 1) * TOKENS] = p
                    e_ref[t * TOKENS : (t + 1) * TOKENS] = p.astype(jnp.bfloat16)
                v_all = jnp.concatenate([keys.at(1, i, j) for i, j in places], axis=0)
                k_all = jnp.concatenate([keys.at(0, i, j) for i, j in places], axis=0)
                att = gather_heads(tn(e_ref[...], v_all)) * own_mark.astype(jnp.float32)
                att = att.astype(jnp.bfloat16)
                put_tile(att_ref, a, b, att.astype(jnp.float32))
                prod = (own_qg[a][1, b].astype(jnp.float32) * att.astype(jnp.float32)).T
                dot = jnp.concatenate(
                    [jnp.sum(prod[h * HEAD : (h + 1) * HEAD], axis=0, keepdims=True) for h in range(PER)],
                    axis=1,
                )
                stat_refs[a][0, b, 0:1] = top + jnp.log2(total)
                stat_refs[a][0, b, 1:2] = dot
                for t, (i, j) in enumerate(places):
                    if 0 <= i < rows and 0 <= j < cols:
                        sum_ref[1, i * cols + j] += nn(e_ref[t * TOKENS : (t + 1) * TOKENS], g)
                for t, (i, j) in enumerate(places):
                    gp = nt(keys.at(1, i, j), g)
                    ds = s_ref[t * TOKENS : (t + 1) * TOKENS] * (gp - dot)
                    e_ref[t * TOKENS : (t + 1) * TOKENS] = ds.astype(jnp.bfloat16)
                put_tile(gq_ref, a, b, gather_heads(tn(e_ref[...], k_all)) * SCALE)
                for t, (i, j) in enumerate(places):
                    if 0 <= i < rows and 0 <= j < cols:
                        sum_ref[0, i * cols + j] += nn(e_ref[t * TOKENS : (t + 1) * TOKENS], q)

    return body


def key_kernel(rows, cols):
    def body(mark_ref, *refs):
        own_kv, refs = refs[:rows], refs[rows:]
        near_qg, refs = refs[:6], refs[6:]
        near_stat, refs = refs[:6], refs[6:]
        sum_ref, gk_ref, gv_ref, acc_ref = refs
        queries = Ext(rows, cols, None, near_qg)
        above_s, below_s, left_s, right_s, corner_left_s, corner_right_s = near_stat
        mask = head_mask()
        acc_ref[...] = sum_ref[...]

        def stat_at(i, j):
            if 0 <= i < rows:
                return (left_s if j < 0 else right_s)[0, i]
            end = 0 if i < 0 else 1
            if j < 0:
                return corner_left_s[0, end]
            if j >= cols:
                return corner_right_s[0, end]
            return (above_s, below_s)[end][0, j]

        for i in range(-1, rows + 1):
            for j in range(-1, cols + 1):
                if 0 <= i < rows and 0 <= j < cols:
                    continue
                places = [
                    (x, y)
                    for x in range(max(i - 1, 0), min(i + 2, rows))
                    for y in range(max(j - 1, 0), min(j + 2, cols))
                ]
                q = spread(queries.at(0, i, j), mask)
                g = spread(queries.at(1, i, j), mask)
                stat = stat_at(i, j)
                own_mark = mark_ref[i + 1, j + 1]
                for x, y in places:
                    allowed = own_mark * mark_ref[x + 1, y + 1] > 0
                    s = nt(own_kv[x][0, y], q)
                    p = jnp.exp2(s * LOG2E - jnp.where(allowed, stat[0:1], BIG))
                    gp = nt(own_kv[x][1, y], g)
                    ds = (p * (gp - stat[1:2])).astype(jnp.bfloat16)
                    acc_ref[1, x * cols + y] += nn(p.astype(jnp.bfloat16), g)
                    acc_ref[0, x * cols + y] += nn(ds, q)
        for x in range(rows):
            for y in range(cols):
                put_tile(gk_ref, x, y, acc_ref[0, x * cols + y])
                put_tile(gv_ref, x, y, acc_ref[1, x * cols + y])

    return body


def tiles_spec(shape):
    return pl.BlockSpec(tuple(shape[:-1]) + (LANES,), lambda g: (0,) * (len(shape) - 1) + (g,))


def stat_spec(shape):
    return pl.BlockSpec((1,) + tuple(shape[1:]), lambda g: (g,) + (0,) * (len(shape) - 1))


def specs(arrays):
    return [tiles_spec(array.shape) for array in arrays]


def local(query_grid, key_grid, value_grid, out_grad, tissue):
    rows, cols = tissue.shape
    width = query_grid.shape[-1]
    groups = width // LANES
    own_kv = pack(key_grid, value_grid, tissue, False)
    near_kv = halo(own_kv[0], own_kv[rows - 1], own_kv[rows], own_kv[rows + 1])
    own_qg = pack(query_grid, out_grad, tissue, True)
    near_qg = halo(own_qg[0], own_qg[rows - 1], own_qg[rows], own_qg[rows + 1])
    marks = tissue
    for axis, dim in (("rows", 0), ("cols", 1)):
        length = marks.shape[dim]
        before = shift(lax.slice_in_dim(marks, length - 1, length, axis=dim), axis, 1)
        after = shift(lax.slice_in_dim(marks, 0, 1, axis=dim), axis, -1)
        marks = jnp.concatenate([before, marks, after], axis=dim)
    own_kv, own_qg = own_kv[:rows], own_qg[:rows]
    grid_out = jax.ShapeDtypeStruct(query_grid.shape, jnp.bfloat16)
    stat_out = jax.ShapeDtypeStruct((groups, cols, 2, LANES), jnp.float32)
    sum_out = jax.ShapeDtypeStruct((2, rows * cols, TOKENS, width), jnp.float32)
    smem = pl.BlockSpec(memory_space=pltpu.SMEM)
    attended, grad_query, *rest = pl.pallas_call(
        query_kernel(rows, cols),
        grid=(groups,),
        in_specs=[smem] + specs(own_kv) + specs(near_kv) + specs(own_qg),
        out_specs=[tiles_spec(grid_out.shape)] * 2 + [stat_spec(stat_out.shape)] * rows + [tiles_spec(sum_out.shape)],
        out_shape=[grid_out] * 2 + [stat_out] * rows + [sum_out],
        scratch_shapes=[pltpu.VMEM((9 * TOKENS, LANES), jnp.float32), pltpu.VMEM((9 * TOKENS, LANES), jnp.bfloat16)],
        compiler_params=pltpu.CompilerParams(vmem_limit_bytes=LIMIT),
    )(marks, *own_kv, *near_kv, *own_qg)
    stats, sums = rest[:rows], rest[rows]
    above = shift(stats[rows - 1], "rows", 1)
    below = shift(stats[0], "rows", -1)
    side = lambda j: jnp.stack([stat[:, j] for stat in stats] + [above[:, j], below[:, j]], axis=1)
    from_left = shift(side(cols - 1), "cols", 1)
    from_right = shift(side(0), "cols", -1)
    near_stat = (above, below, from_left[:, :rows], from_right[:, :rows], from_left[:, rows:], from_right[:, rows:])
    grad_key, grad_value = pl.pallas_call(
        key_kernel(rows, cols),
        grid=(groups,),
        in_specs=[smem] + specs(own_kv) + specs(near_qg) + [stat_spec(s.shape) for s in near_stat] + [tiles_spec(sums.shape)],
        out_specs=[tiles_spec(grid_out.shape)] * 2,
        out_shape=[grid_out] * 2,
        scratch_shapes=[pltpu.VMEM((2, rows * cols, TOKENS, LANES), jnp.float32)],
        compiler_params=pltpu.CompilerParams(vmem_limit_bytes=LIMIT),
    )(marks, *own_kv, *near_qg, *near_stat, sums)
    return attended, grad_query, grad_key, grad_value


def solution(mesh):
    grid = P(("groups", "rows"), "cols", None)
    return jax.shard_map(
        local,
        mesh=mesh,
        in_specs=(grid, grid, grid, grid, P(("groups", "rows"), "cols")),
        out_specs=(grid, grid, grid, grid),
        check_vma=False,
    )
```

```python
import jax
import jax.numpy as jnp
from jax import lax
from jax.experimental import pallas as pl
from jax.experimental.pallas import tpu as pltpu
from jax.sharding import PartitionSpec as P

HEAD = 64
TILE = 8
TOKENS = TILE * TILE
LANES = 256
PER = LANES // HEAD
MARKS = 16
SCALE = HEAD ** -0.5
LOG2E = 1.4426950408889634
NEG = -1e30
BIG = 1e30
LIMIT = 56 * 1024 * 1024
VMEM = pl.BlockSpec(memory_space=pltpu.VMEM)
SMEM = pl.BlockSpec(memory_space=pltpu.SMEM)
BF16 = jnp.bfloat16
F32 = jnp.float32


def shift(array, axis, by):
    count = lax.axis_size(axis)
    pairs = [(i, i + by) for i in range(count) if 0 <= i + by < count]
    return lax.ppermute(array, axis, pairs)


def nt(a, b):
    return lax.dot_general(a, b, (((1,), (1,)), ((), ())), preferred_element_type=F32)


def nn(a, b):
    return lax.dot_general(a, b, (((1,), (0,)), ((), ())), preferred_element_type=F32)


def tn(a, b):
    return lax.dot_general(a, b, (((0,), (0,)), ((), ())), preferred_element_type=F32)


def call(body, out_shape, args, marks_first=True, flops=0, exps=0):
    size = sum(array.size * array.dtype.itemsize for array in args)
    return pl.pallas_call(
        body,
        in_specs=[SMEM if marks_first and n == 0 else VMEM for n in range(len(args))],
        out_specs=[VMEM] * len(out_shape),
        out_shape=out_shape,
        compiler_params=pltpu.CompilerParams(vmem_limit_bytes=LIMIT),
        cost_estimate=pl.CostEstimate(flops=flops, transcendentals=exps, bytes_accessed=size),
    )(*args)


def tile_of(ref, a, b):
    block = ref[TILE * a : TILE * (a + 1), TILE * b : TILE * (b + 1), :]
    return block.astype(F32).reshape(TOKENS, block.shape[-1])


def put_tile(ref, a, b, lanes, value):
    shaped = value.reshape(TILE, TILE, value.shape[-1]).astype(ref.dtype)
    ref[TILE * a : TILE * (a + 1), TILE * b : TILE * (b + 1), lanes] = shaped


def rows_of(index):
    return slice(index * TOKENS, (index + 1) * TOKENS)


def mark_row(ref, start, index, lanes):
    return ref[start : start + MARKS, lanes].astype(F32)[index : index + 1]


def pack(first, second, tissue, scaled):
    rows, cols = tissue.shape
    width = first.shape[-1]

    def body(mark_ref, first_ref, second_ref, *row_refs):
        for a in range(rows):
            for b in range(cols):
                mark = mark_ref[a, b].astype(F32)
                for n, ref in enumerate((first_ref, second_ref)):
                    tile = tile_of(ref, a, b)
                    if scaled:
                        tile = tile * (SCALE if n == 0 else mark)
                    row_refs[a][rows_of(n * cols + b), :] = tile.astype(BF16)
            if not scaled:
                which = lax.broadcasted_iota(jnp.int32, (MARKS, width), 0)
                marks = jnp.zeros((MARKS, width), F32)
                for b in range(cols):
                    marks = jnp.where(which == b, mark_ref[a, b].astype(F32), marks)
                row_refs[a][2 * cols * TOKENS :, :] = marks.astype(BF16)

    height = 2 * cols * TOKENS + (0 if scaled else MARKS)
    shape = jax.ShapeDtypeStruct((height, width), BF16)
    return call(body, [shape] * rows, (tissue, first, second))


def pack_sides(own_kv, own_qg, cols):
    rows = len(own_kv)
    width = own_kv[0].shape[1]

    def body(*refs):
        kv, qg, outs = refs[:rows], refs[rows : 2 * rows], refs[2 * rows :]
        for b, out in zip((0, cols - 1), outs):
            for n in range(4):
                src = kv if n < 2 else qg
                for a in range(rows):
                    out[rows_of(n * rows + a), :] = src[a][rows_of((n % 2) * cols + b), :]
            which = lax.broadcasted_iota(jnp.int32, (MARKS, width), 0)
            marks = jnp.zeros((MARKS, width), F32)
            for a in range(rows):
                marks = jnp.where(which == a, mark_row(kv[a], 2 * cols * TOKENS, b, slice(None)), marks)
            out[4 * rows * TOKENS :, :] = marks.astype(BF16)

    shape = jax.ShapeDtypeStruct((4 * rows * TOKENS + MARKS, width), BF16)
    return call(body, [shape] * 2, (*own_kv, *own_qg), marks_first=False)


def pack_corners(above, below, cols, marked):
    width = above.shape[1]

    def body(above_ref, below_ref, *outs):
        for b, out in zip((0, cols - 1), outs):
            for n in range(2):
                for end, ref in enumerate((above_ref, below_ref)):
                    out[rows_of(n * 2 + end), :] = ref[rows_of(n * cols + b), :]
            if marked:
                which = lax.broadcasted_iota(jnp.int32, (MARKS, width), 0)
                marks = jnp.zeros((MARKS, width), F32)
                for end, ref in enumerate((above_ref, below_ref)):
                    marks = jnp.where(which == end, mark_row(ref, 2 * cols * TOKENS, b, slice(None)), marks)
                out[4 * TOKENS :, :] = marks.astype(BF16)

    shape = jax.ShapeDtypeStruct((4 * TOKENS + (MARKS if marked else 0), width), BF16)
    return call(body, [shape] * 2, (above, below), marks_first=False)


def pack_stats(own, above, below, cols):
    rows = len(own)

    def body(*refs):
        sources, outs = refs[: rows + 2], refs[rows + 2 :]
        for b, out in zip((0, cols - 1), outs):
            for n, ref in enumerate(sources):
                out[2 * n : 2 * n + 2, :] = ref[2 * b : 2 * b + 2, :]

    shape = jax.ShapeDtypeStruct((2 * (rows + 2), own[0].shape[1]), F32)
    return call(body, [shape] * 2, (*own, above, below), marks_first=False)


def head_mask():
    row = lax.broadcasted_iota(jnp.int32, (LANES, LANES), 0) // HEAD
    lane = lax.broadcasted_iota(jnp.int32, (LANES, LANES), 1) // HEAD
    return row == lane


def spread(tile, mask):
    return jnp.where(mask, jnp.concatenate([tile] * PER, axis=0), jnp.zeros((), tile.dtype))


def gather_heads(full):
    lane = lax.broadcasted_iota(jnp.int32, (TOKENS, LANES), 1) // HEAD
    out = full[:TOKENS]
    for h in range(1, PER):
        out = jnp.where(lane == h, full[h * TOKENS : (h + 1) * TOKENS], out)
    return out


def fold(x, op):
    return op(x.reshape(x.shape[0] // 8, 8, x.shape[1]), axis=0)


class Block:
    def __init__(self, rows, cols, own, near, lanes):
        self.rows, self.cols, self.own, self.lanes = rows, cols, own, lanes
        self.above, self.below, self.left, self.right, self.corner_left, self.corner_right = near

    def tile(self, n, i, j, side):
        ends = {-1: (self.above, 0), self.rows: (self.below, 1)}
        if 0 <= j < self.cols:
            ref = ends[i][0] if i in ends else self.own[i]
            return ref[rows_of(n * self.cols + j), self.lanes]
        if i in ends:
            ref = self.corner_left if j < 0 else self.corner_right
            return ref[rows_of(n * 2 + ends[i][1]), self.lanes]
        ref = self.left if j < 0 else self.right
        return ref[rows_of((side + n) * self.rows + i), self.lanes]

    def mark(self, marks, i, j):
        ends = {-1: (self.above, 0), self.rows: (self.below, 1)}
        if 0 <= j < self.cols:
            if i not in ends:
                return marks[i, j].astype(F32)
            return mark_row(ends[i][0], 2 * self.cols * TOKENS, j, self.lanes)
        if i in ends:
            ref = self.corner_left if j < 0 else self.corner_right
            return mark_row(ref, 4 * TOKENS, ends[i][1], self.lanes)
        ref = self.left if j < 0 else self.right
        return mark_row(ref, 4 * self.rows * TOKENS, i, self.lanes)


def around(a, b):
    return [(a + i, b + j) for j in (-1, 0, 1) for i in (-1, 0, 1)]


def each_group(width, step):
    def one(g, carry):
        step(pl.ds(pl.multiple_of(g * LANES, LANES), LANES))
        return carry

    lax.fori_loop(0, width // LANES, one, 0)


def forward(rows, cols, width):
    def body(mark_ref, *refs):
        own_kv, near, own_qg = refs[:rows], refs[rows : rows + 6], refs[rows + 6 : 2 * rows + 6]
        att_ref, *stat_refs = refs[2 * rows + 6 :]
        mask = head_mask()

        def step(lanes):
            block = Block(rows, cols, own_kv, near, lanes)
            for a in range(rows):
                for b in range(cols):
                    places = around(a, b)
                    own_mark = mark_ref[a, b].astype(F32)
                    allowed = [
                        None if place == (a, b) else own_mark * block.mark(mark_ref, *place) > 0
                        for place in places
                    ]
                    q = spread(own_qg[a][rows_of(b), lanes], mask)
                    keys = jnp.concatenate([block.tile(0, i, j, 0) for i, j in places], axis=0)
                    values = jnp.concatenate([block.tile(1, i, j, 0) for i, j in places], axis=0)
                    scores = nt(keys, q)
                    top = None
                    for t, ok in enumerate(allowed):
                        high = fold(scores[rows_of(t)], jnp.max)
                        if ok is not None:
                            high = jnp.where(ok, high, NEG)
                        top = high if top is None else jnp.maximum(top, high)
                    top = jnp.max(top, axis=0, keepdims=True) * LOG2E
                    total = jnp.zeros((8, LANES), F32)
                    low = []
                    for t, ok in enumerate(allowed):
                        less = top if ok is None else jnp.where(ok, top, BIG)
                        e = jnp.exp2(scores[rows_of(t)] * LOG2E - less)
                        total = total + fold(e, jnp.sum)
                        low.append(e.astype(BF16))
                    total = jnp.sum(total, axis=0, keepdims=True)
                    inverse = jnp.broadcast_to(own_mark / total, (8, LANES)).T[:, :1]
                    att = gather_heads(tn(jnp.concatenate(low, axis=0), values) * inverse).astype(BF16).astype(F32)
                    put_tile(att_ref, a, b, lanes, att)
                    prod = (own_qg[a][rows_of(cols + b), lanes].astype(F32) * att).T
                    dot = [jnp.sum(prod[rows_of(h)], axis=0, keepdims=True) for h in range(PER)]
                    stat_refs[a][2 * b : 2 * b + 1, lanes] = top + jnp.log2(total)
                    stat_refs[a][2 * b + 1 : 2 * b + 2, lanes] = jnp.concatenate(dot, axis=1)

        each_group(width, step)

    return body


def backward(rows, cols, width):
    def body(mark_ref, *refs):
        own_kv, near, own_qg = refs[:rows], refs[rows : rows + 6], refs[rows + 6 : 2 * rows + 6]
        stat_refs = refs[2 * rows + 6 : 3 * rows + 6]
        gq_ref, sum_ref = refs[3 * rows + 6 :]
        mask = head_mask()
        sum_ref[...] = jnp.zeros(sum_ref.shape, F32)

        def step(lanes):
            block = Block(rows, cols, own_kv, near, lanes)
            for a in range(rows):
                for b in range(cols):
                    places = around(a, b)
                    own_mark = mark_ref[a, b].astype(F32)
                    q = spread(own_qg[a][rows_of(b), lanes], mask)
                    g = spread(own_qg[a][rows_of(cols + b), lanes], mask)
                    keys = jnp.concatenate([block.tile(0, i, j, 0) for i, j in places], axis=0)
                    values = jnp.concatenate([block.tile(1, i, j, 0) for i, j in places], axis=0)
                    level = stat_refs[a][2 * b : 2 * b + 1, lanes]
                    dot = stat_refs[a][2 * b + 1 : 2 * b + 2, lanes]
                    scores, grads = nt(keys, q), nt(values, g)
                    probs, slopes = [], []
                    for t, place in enumerate(places):
                        less = level
                        if place != (a, b):
                            less = jnp.where(own_mark * block.mark(mark_ref, *place) > 0, level, BIG)
                        p = jnp.exp2(scores[rows_of(t)] * LOG2E - less)
                        probs.append(p.astype(BF16))
                        slopes.append((p * (grads[rows_of(t)] - dot)).astype(BF16))
                    gq = gather_heads(tn(jnp.concatenate(slopes, axis=0), keys)) * SCALE
                    put_tile(gq_ref, a, b, lanes, gq)
                    inside = [t for t, (i, j) in enumerate(places) if 0 <= i < rows and 0 <= j < cols]
                    for n, (parts, right) in enumerate(((slopes, q), (probs, g))):
                        part = nn(jnp.concatenate([parts[t] for t in inside], axis=0), right)
                        for u, t in enumerate(inside):
                            i, j = places[t]
                            sum_ref[n, rows_of(i * cols + j), lanes] += part[rows_of(u)]

        each_group(width, step)

    return body


def key_side(rows, cols, width):
    def body(mark_ref, *refs):
        own_kv, near_kv, near_qg = refs[:rows], refs[rows : rows + 6], refs[rows + 6 : rows + 12]
        above_s, below_s, left_s, right_s, sum_ref, gk_ref, gv_ref, acc_ref = refs[rows + 12 :]
        mask = head_mask()
        acc_ref[...] = sum_ref[...]

        def stat_at(i, j, lanes):
            if 0 <= j < cols:
                ref, start = (above_s if i < 0 else below_s), j
            else:
                ref, start = (left_s if j < 0 else right_s), (rows if i < 0 else rows + 1 if i >= rows else i)
            return ref[2 * start : 2 * start + 1, lanes], ref[2 * start + 1 : 2 * start + 2, lanes]

        def step(lanes):
            marks = Block(rows, cols, own_kv, near_kv, lanes)
            queries = Block(rows, cols, None, near_qg, lanes)
            for i in range(-1, rows + 1):
                for j in range(-1, cols + 1):
                    if 0 <= i < rows and 0 <= j < cols:
                        continue
                    places = [(x, y) for x, y in around(i, j) if 0 <= x < rows and 0 <= y < cols]
                    q = spread(queries.tile(0, i, j, 2), mask)
                    g = spread(queries.tile(1, i, j, 2), mask)
                    level, dot = stat_at(i, j, lanes)
                    mark = marks.mark(mark_ref, i, j)
                    keys = jnp.concatenate([marks.tile(0, x, y, 0) for x, y in places], axis=0)
                    values = jnp.concatenate([marks.tile(1, x, y, 0) for x, y in places], axis=0)
                    scores, grads = nt(keys, q), nt(values, g)
                    probs, slopes = [], []
                    for t, (x, y) in enumerate(places):
                        less = jnp.where(mark * mark_ref[x, y].astype(F32) > 0, level, BIG)
                        p = jnp.exp2(scores[rows_of(t)] * LOG2E - less)
                        probs.append(p.astype(BF16))
                        slopes.append((p * (grads[rows_of(t)] - dot)).astype(BF16))
                    for n, (parts, right) in enumerate(((slopes, q), (probs, g))):
                        part = nn(jnp.concatenate(parts, axis=0), right)
                        for t, (x, y) in enumerate(places):
                            acc_ref[n, rows_of(x * cols + y), lanes] += part[rows_of(t)]
            for x in range(rows):
                for y in range(cols):
                    put_tile(gk_ref, x, y, lanes, acc_ref[0, rows_of(x * cols + y), lanes])
                    put_tile(gv_ref, x, y, lanes, acc_ref[1, rows_of(x * cols + y), lanes])

        each_group(width, step)

    return body


def local(query_grid, key_grid, value_grid, out_grad, tissue):
    rows, cols = tissue.shape
    width = query_grid.shape[-1]
    own_kv = pack(key_grid, value_grid, tissue, False)
    above_kv = shift(own_kv[-1], "rows", 1)
    below_kv = shift(own_kv[0], "rows", -1)
    own_qg = pack(query_grid, out_grad, tissue, True)
    above_qg = shift(own_qg[-1], "rows", 1)
    below_qg = shift(own_qg[0], "rows", -1)
    first_side, last_side = pack_sides(own_kv, own_qg, cols)
    left = shift(last_side, "cols", 1)
    right = shift(first_side, "cols", -1)
    first_kv, last_kv = pack_corners(above_kv, below_kv, cols, True)
    near_kv = (above_kv, below_kv, left, right, shift(last_kv, "cols", 1), shift(first_kv, "cols", -1))
    grid_out = jax.ShapeDtypeStruct(query_grid.shape, BF16)
    stat_out = jax.ShapeDtypeStruct((2 * cols, width), F32)
    sum_out = jax.ShapeDtypeStruct((2, rows * cols * TOKENS, width), F32)
    pairs = 9 * rows * cols * TOKENS * TOKENS * width
    attended, *stats = call(
        forward(rows, cols, width), [grid_out] + [stat_out] * rows,
        (tissue, *own_kv, *near_kv, *own_qg), flops=16 * pairs, exps=pairs // HEAD,
    )
    above_s = shift(stats[-1], "rows", 1)
    below_s = shift(stats[0], "rows", -1)
    first_s, last_s = pack_stats(stats, above_s, below_s, cols)
    left_s = shift(last_s, "cols", 1)
    right_s = shift(first_s, "cols", -1)
    first_qg, last_qg = pack_corners(above_qg, below_qg, cols, False)
    near_qg = (above_qg, below_qg, left, right, shift(last_qg, "cols", 1), shift(first_qg, "cols", -1))
    grad_query, sums = call(
        backward(rows, cols, width), [grid_out, sum_out],
        (tissue, *own_kv, *near_kv, *own_qg, *stats), flops=32 * pairs, exps=pairs // HEAD,
    )
    args = (tissue, *own_kv, *near_kv, *near_qg, above_s, below_s, left_s, right_s, sums)
    grad_key, grad_value = pl.pallas_call(
        key_side(rows, cols, width),
        in_specs=[SMEM] + [VMEM] * (len(args) - 1),
        out_specs=[VMEM] * 2,
        out_shape=[grid_out] * 2,
        scratch_shapes=[pltpu.VMEM(sum_out.shape, F32)],
        compiler_params=pltpu.CompilerParams(vmem_limit_bytes=LIMIT),
        cost_estimate=pl.CostEstimate(flops=8 * pairs, transcendentals=pairs // (2 * HEAD), bytes_accessed=1 << 20),
    )(*args)
    return attended, grad_query, grad_key, grad_value


def solution(mesh):
    grid = P(("groups", "rows"), "cols", None)
    return jax.shard_map(
        local,
        mesh=mesh,
        in_specs=(grid, grid, grid, grid, P(("groups", "rows"), "cols")),
        out_specs=(grid, grid, grid, grid),
        check_vma=False,
    )
```

```python
import jax
import jax.numpy as jnp
from jax import lax
from jax.experimental import pallas as pl
from jax.experimental.pallas import tpu as pltpu
from jax.sharding import PartitionSpec as P

HEAD = 64
TILE = 8
TOKENS = TILE * TILE
LANES = 256
PER = LANES // HEAD
MARKS = 16
SCALE = HEAD ** -0.5
LOG2E = 1.4426950408889634
NEG = -1e30
BIG = 1e30
LIMIT = 20 * 1024 * 1024
VMEM = pl.BlockSpec(memory_space=pltpu.VMEM)
SMEM = pl.BlockSpec(memory_space=pltpu.SMEM)
BF16 = jnp.bfloat16
F32 = jnp.float32


def shift(array, axis, by):
    count = lax.axis_size(axis)
    pairs = [(i, i + by) for i in range(count) if 0 <= i + by < count]
    return lax.ppermute(array, axis, pairs)


def nt(a, b):
    return lax.dot_general(a, b, (((1,), (1,)), ((), ())), preferred_element_type=F32)


def nn(a, b):
    return lax.dot_general(a, b, (((1,), (0,)), ((), ())), preferred_element_type=F32)


def tn(a, b):
    return lax.dot_general(a, b, (((0,), (0,)), ((), ())), preferred_element_type=F32)


def call(body, out_shape, args, marks_first=True, flops=0, exps=0):
    size = sum(array.size * array.dtype.itemsize for array in args)
    return pl.pallas_call(
        body,
        in_specs=[SMEM if marks_first and n == 0 else VMEM for n in range(len(args))],
        out_specs=[VMEM] * len(out_shape),
        out_shape=out_shape,
        compiler_params=pltpu.CompilerParams(vmem_limit_bytes=LIMIT),
        cost_estimate=pl.CostEstimate(flops=flops, transcendentals=exps, bytes_accessed=size),
    )(*args)


def tile_of(ref, a, b):
    block = ref[TILE * a : TILE * (a + 1), TILE * b : TILE * (b + 1), :]
    return block.astype(F32).reshape(TOKENS, block.shape[-1])


def put_tile(ref, a, b, lanes, value):
    shaped = value.reshape(TILE, TILE, value.shape[-1]).astype(ref.dtype)
    ref[TILE * a : TILE * (a + 1), TILE * b : TILE * (b + 1), lanes] = shaped


def rows_of(index):
    return slice(index * TOKENS, (index + 1) * TOKENS)


def mark_row(ref, start, index, lanes):
    return ref[start : start + MARKS, lanes].astype(F32)[index : index + 1]


def write_marks(out, start, marks, width):
    which = lax.broadcasted_iota(jnp.int32, (MARKS, width), 0)
    rows = jnp.zeros((MARKS, width), F32)
    for n, mark in enumerate(marks):
        rows = jnp.where(which == n, mark, rows)
    out[start : start + MARKS, :] = rows.astype(BF16)


def pack(grids, tissue):
    rows, cols = tissue.shape
    width = grids[0].shape[-1]

    def body(mark_ref, *refs):
        sources, refs = refs[:4], refs[4:]
        kv_refs, qg_refs, side_refs = refs[:rows], refs[rows : 2 * rows], refs[2 * rows : 2 * rows + 2]
        grid_refs, sems = refs[2 * rows + 2 : 2 * rows + 6], refs[2 * rows + 6]

        def copies(a):
            span = slice(TILE * a, TILE * (a + 1))
            return [
                pltpu.make_async_copy(source.at[span], ref.at[span], sems.at[a, n])
                for n, (source, ref) in enumerate(zip(sources, grid_refs))
            ]

        for a in range(rows):
            for copy in copies(a):
                copy.start()
        for a in range(rows):
            for copy in copies(a):
                copy.wait()
            marks = [mark_ref[a, b].astype(F32) for b in range(cols)]
            for n, ref in enumerate(grid_refs):
                out = (kv_refs if n < 2 else qg_refs)[a]
                for b in range(cols):
                    tile = tile_of(ref, a, b)
                    if n >= 2:
                        tile = tile * (SCALE if n == 2 else marks[b])
                    tile = tile.astype(BF16)
                    out[rows_of(n % 2 * cols + b), :] = tile
                    for end, side in zip((0, cols - 1), side_refs):
                        if b == end:
                            side[rows_of(n * rows + a), :] = tile
            write_marks(kv_refs[a], 2 * cols * TOKENS, marks, width)
        for b, side in zip((0, cols - 1), side_refs):
            write_marks(side, 4 * rows * TOKENS, [mark_ref[a, b].astype(F32) for a in range(rows)], width)

    shapes = [2 * cols * TOKENS + MARKS] * rows + [2 * cols * TOKENS] * rows + [4 * rows * TOKENS + MARKS] * 2
    shapes = [jax.ShapeDtypeStruct((height, width), BF16) for height in shapes]
    outs = pl.pallas_call(
        body,
        in_specs=[SMEM] + [pl.BlockSpec(memory_space=pltpu.HBM)] * 4,
        out_specs=[VMEM] * len(shapes),
        out_shape=shapes,
        scratch_shapes=[pltpu.VMEM(grid.shape, grid.dtype) for grid in grids] + [pltpu.SemaphoreType.DMA((rows, 4))],
        compiler_params=pltpu.CompilerParams(vmem_limit_bytes=LIMIT),
        cost_estimate=pl.CostEstimate(flops=0, transcendentals=0, bytes_accessed=1 << 20),
    )(tissue, *(pltpu.with_memory_space_constraint(grid, pltpu.HBM) for grid in grids))
    return outs[:rows], outs[rows : 2 * rows], outs[2 * rows :]


def pack_corners(above, below, cols):
    width = above.shape[1]

    def body(above_ref, below_ref, *outs):
        for b, out in zip((0, cols - 1), outs):
            for n in range(2):
                for end, ref in enumerate((above_ref, below_ref)):
                    out[rows_of(n * 2 + end), :] = ref[rows_of(n * cols + b), :]
            ends = [mark_row(ref, 2 * cols * TOKENS, b, slice(None)) for ref in (above_ref, below_ref)]
            write_marks(out, 4 * TOKENS, ends, width)

    shape = jax.ShapeDtypeStruct((4 * TOKENS + MARKS, width), BF16)
    return call(body, [shape] * 2, (above, below), marks_first=False)


def pieces(x):
    out = []
    for _ in range(3):
        out.append(x.astype(BF16))
        x = x - out[-1].astype(F32)
    return out


def pack_queries(stats, above_s, below_s, above_qg, below_qg, cols):
    rows = len(stats)
    width = above_s.shape[1]
    height = -(-6 * (rows + 2) // MARKS) * MARKS

    def body(*refs):
        stat_refs, ends, outs = refs[: rows + 2], refs[rows + 2 : rows + 4], refs[rows + 4 :]
        for b, out in zip((0, cols - 1), outs):
            for n in range(2):
                for end, ref in enumerate(ends):
                    out[rows_of(n * 2 + end), :] = ref[rows_of(n * cols + b), :]
            parts = pieces(jnp.concatenate([ref[2 * b : 2 * b + 2, :] for ref in stat_refs], axis=0))
            parts = [part.astype(F32) for part in parts]
            rest = height - 6 * (rows + 2)
            if rest:
                parts.append(jnp.zeros((rest, width), F32))
            out[4 * TOKENS :, :] = jnp.concatenate(parts, axis=0).astype(BF16)

    shape = jax.ShapeDtypeStruct((4 * TOKENS + height, width), BF16)
    return call(body, [shape] * 2, (*stats, above_s, below_s, above_qg, below_qg), marks_first=False)


def head_mask():
    row = lax.broadcasted_iota(jnp.int32, (LANES, LANES), 0) // HEAD
    lane = lax.broadcasted_iota(jnp.int32, (LANES, LANES), 1) // HEAD
    return row == lane


def spread(tile, mask):
    return jnp.where(mask, jnp.concatenate([tile] * PER, axis=0), jnp.zeros((), tile.dtype))


def gather_heads(full):
    lane = lax.broadcasted_iota(jnp.int32, (TOKENS, LANES), 1) // HEAD
    out = full[:TOKENS]
    for h in range(1, PER):
        out = jnp.where(lane == h, full[h * TOKENS : (h + 1) * TOKENS], out)
    return out


def fold(x, op):
    return op(x.reshape(x.shape[0] // 8, 8, x.shape[1]), axis=0)


class Block:
    def __init__(self, rows, cols, own, near, lanes):
        self.rows, self.cols, self.own, self.lanes = rows, cols, own, lanes
        self.above, self.below, self.left, self.right, self.corner_left, self.corner_right = near

    def tile(self, n, i, j, side):
        ends = {-1: (self.above, 0), self.rows: (self.below, 1)}
        if 0 <= j < self.cols:
            ref = ends[i][0] if i in ends else self.own[i]
            return ref[rows_of(n * self.cols + j), self.lanes]
        if i in ends:
            ref = self.corner_left if j < 0 else self.corner_right
            return ref[rows_of(n * 2 + ends[i][1]), self.lanes]
        ref = self.left if j < 0 else self.right
        return ref[rows_of((side + n) * self.rows + i), self.lanes]

    def mark(self, marks, i, j):
        ends = {-1: (self.above, 0), self.rows: (self.below, 1)}
        if 0 <= j < self.cols:
            if i not in ends:
                return marks[i, j].astype(F32)
            return mark_row(ends[i][0], 2 * self.cols * TOKENS, j, self.lanes)
        if i in ends:
            ref = self.corner_left if j < 0 else self.corner_right
            return mark_row(ref, 4 * TOKENS, ends[i][1], self.lanes)
        ref = self.left if j < 0 else self.right
        return mark_row(ref, 4 * self.rows * TOKENS, i, self.lanes)


def drive(programs):
    active = list(programs)
    while active:
        active = [program for program in active if next(program, True) is None]


def around(a, b):
    return [(a + i, b + j) for j in (-1, 0, 1) for i in (-1, 0, 1)]


def each_group(width, step):
    def one(g, carry):
        step(pl.ds(pl.multiple_of(g * LANES, LANES), LANES))
        return carry

    lax.fori_loop(0, width // LANES, one, 0)


def columns(first, second):
    rows = jnp.concatenate(
        [part.astype(F32) for row in (first, second) for part in pieces(row) + [jnp.zeros_like(row)] * 5], axis=0
    )
    index = lax.broadcasted_iota(jnp.int32, (MARKS, LANES), 0) // 8
    lane = lax.broadcasted_iota(jnp.int32, (MARKS, LANES), 1) // 128
    full = tn(rows.astype(BF16), jnp.where(index == lane, 1.0, 0.0).astype(BF16))
    return [
        gather_heads(jnp.concatenate([full[:, 128 * n : 128 * (n + 1)]] * (LANES // 128), axis=1)) for n in range(2)
    ]


def softmax_part(scores, allowed, top):
    for t, ok in enumerate(allowed):
        high = fold(scores[rows_of(t)], jnp.max)
        if ok is not None:
            high = jnp.where(ok, high, NEG)
        high = high * LOG2E
        top = high if top is None else jnp.maximum(top, high)
    return jnp.max(top, axis=0, keepdims=True)


def exponentials(scores, allowed, top):
    total = jnp.zeros((8, LANES), F32)
    low = []
    for t, ok in enumerate(allowed):
        less = top if ok is None else jnp.where(ok, top, BIG)
        e = jnp.exp2(scores[rows_of(t)] * LOG2E - less)
        total = total + fold(e, jnp.sum)
        low.append(e.astype(BF16))
    return jnp.concatenate(low, axis=0), jnp.sum(total, axis=0, keepdims=True)


def split_places(a, b, rows, cols):
    inside = [(i, j) for i, j in around(a, b) if 0 <= i < rows and 0 <= j < cols]
    return inside, [place for place in around(a, b) if place not in inside]


def forward_own(rows, cols, width):
    def body(mark_ref, *refs):
        own_kv, own_qg = refs[:rows], refs[rows : 2 * rows]
        part_ref, level_ref = refs[2 * rows :]
        mask = head_mask()

        def tile(block, lanes, a, b):
            places, _ = split_places(a, b, rows, cols)
            allowed = [None if place == (a, b) else mark_ref[a, b] * mark_ref[place] > 0 for place in places]
            q = spread(own_qg[a][rows_of(b), lanes], mask)
            scores = nt(jnp.concatenate([block.tile(0, i, j, 0) for i, j in places], axis=0), q)
            yield
            top = softmax_part(scores, allowed, None)
            yield
            low, total = exponentials(scores, allowed, top)
            yield
            full = tn(low, jnp.concatenate([block.tile(1, i, j, 0) for i, j in places], axis=0))
            yield
            index = a * cols + b
            part_ref[rows_of(index), lanes] = gather_heads(full)
            level_ref[2 * index : 2 * index + 1, lanes] = top
            level_ref[2 * index + 1 : 2 * index + 2, lanes] = total

        def step(lanes):
            block = Block(rows, cols, own_kv, (None,) * 6, lanes)
            drive(tile(block, lanes, a, b) for a in range(rows) for b in range(cols))

        each_group(width, step)

    return body


def forward(rows, cols, width):
    def body(mark_ref, *refs):
        own_kv, near, own_qg = refs[:rows], refs[rows : rows + 6], refs[rows + 6 : 2 * rows + 6]
        part_ref, level_ref, att_ref, *stat_refs = refs[2 * rows + 6 :]
        mask = head_mask()

        def tile(block, lanes, a, b):
            _, places = split_places(a, b, rows, cols)
            index = a * cols + b
            own_mark = mark_ref[a, b].astype(F32)
            allowed = [own_mark * block.mark(mark_ref, *place) > 0 for place in places]
            q = spread(own_qg[a][rows_of(b), lanes], mask)
            scores = nt(jnp.concatenate([block.tile(0, i, j, 0) for i, j in places], axis=0), q)
            yield
            first = level_ref[2 * index : 2 * index + 1, lanes]
            top = softmax_part(scores, allowed, jnp.broadcast_to(first, (8, LANES)))
            yield
            low, total = exponentials(scores, allowed, top)
            less = jnp.exp2(first - top)
            total = total + less * level_ref[2 * index + 1 : 2 * index + 2, lanes]
            yield
            full = tn(low, jnp.concatenate([block.tile(1, i, j, 0) for i, j in places], axis=0))
            inverse = own_mark / total
            near_by, own_by = columns(inverse, inverse * less)
            yield
            att = (gather_heads(full) * near_by + part_ref[rows_of(index), lanes] * own_by).astype(BF16).astype(F32)
            put_tile(att_ref, a, b, lanes, att)
            prod = (own_qg[a][rows_of(cols + b), lanes].astype(F32) * att).T
            dot = [jnp.sum(prod[rows_of(h)], axis=0, keepdims=True) for h in range(PER)]
            stat_refs[a][2 * b : 2 * b + 1, lanes] = top + jnp.log2(total)
            stat_refs[a][2 * b + 1 : 2 * b + 2, lanes] = jnp.concatenate(dot, axis=1)

        def step(lanes):
            block = Block(rows, cols, own_kv, near, lanes)
            drive(tile(block, lanes, a, b) for a in range(rows) for b in range(cols))

        each_group(width, step)

    return body


def backward(rows, cols, width, a):
    def body(mark_ref, *refs):
        all_refs = refs
        own_kv, near, own_qg = refs[:rows], refs[rows : rows + 6], refs[rows + 6 : 2 * rows + 6]
        stat_ref, refs = refs[2 * rows + 6], refs[2 * rows + 7 + (2 if a else 0) :]
        before_ref = None if a == 0 else all_refs[2 * rows + 8]
        gq_ref, sum_ref, out_ref, sem = refs
        mask = head_mask()
        sum_ref[...] = jnp.zeros(sum_ref.shape, F32) if a == 0 else before_ref[...]

        def tile(block, lanes, b):
            places = around(a, b)
            own_mark = mark_ref[a, b].astype(F32)
            q = spread(own_qg[a][rows_of(b), lanes], mask)
            g = spread(own_qg[a][rows_of(cols + b), lanes], mask)
            keys = jnp.concatenate([block.tile(0, i, j, 0) for i, j in places], axis=0)
            values = jnp.concatenate([block.tile(1, i, j, 0) for i, j in places], axis=0)
            level = stat_ref[2 * b : 2 * b + 1, lanes]
            dot = stat_ref[2 * b + 1 : 2 * b + 2, lanes]
            scores, grads = nt(keys, q), nt(values, g)
            yield
            probs, slopes = [], []
            for t, place in enumerate(places):
                less = level
                if place != (a, b):
                    less = jnp.where(own_mark * block.mark(mark_ref, *place) > 0, level, BIG)
                p = jnp.exp2(scores[rows_of(t)] * LOG2E - less)
                probs.append(p.astype(BF16))
                slopes.append((p * (grads[rows_of(t)] - dot)).astype(BF16))
            yield
            gq = gather_heads(tn(jnp.concatenate(slopes, axis=0), keys)) * SCALE
            put_tile(out_ref, 0, b, lanes, gq)
            inside = [t for t, (i, j) in enumerate(places) if 0 <= i < rows and 0 <= j < cols]
            for n, (parts, right) in enumerate(((slopes, q), (probs, g))):
                part = nn(jnp.concatenate([parts[t] for t in inside], axis=0), right)
                for u, t in enumerate(inside):
                    i, j = places[t]
                    sum_ref[n, rows_of(i * cols + j), lanes] += part[rows_of(u)]

        def step(lanes):
            block = Block(rows, cols, own_kv, near, lanes)
            drive(tile(block, lanes, b) for b in range(cols))

        each_group(width, step)
        copy = pltpu.make_async_copy(out_ref, gq_ref.at[TILE * a : TILE * (a + 1)], sem)
        copy.start()
        copy.wait()

    return body


def key_side(rows, cols, width):
    def body(mark_ref, *refs):
        own_kv, near_kv, near_qg = refs[:rows], refs[rows : rows + 6], refs[rows + 6 : rows + 12]
        above_s, below_s, sum_ref, gk_ref, gv_ref, acc_ref = refs[rows + 12 :]
        mask = head_mask()
        acc_ref[...] = sum_ref[...]

        def stat_at(i, j, lanes):
            if 0 <= j < cols:
                ref = above_s if i < 0 else below_s
                return ref[2 * j : 2 * j + 1, lanes], ref[2 * j + 1 : 2 * j + 2, lanes]
            ref = near_qg[4 if j < 0 else 5]
            parts = ref[4 * TOKENS :, lanes].astype(F32)
            count = 2 * (rows + 2)
            stats = parts[:count] + parts[count : 2 * count] + parts[2 * count : 3 * count]
            n = rows if i < 0 else rows + 1 if i >= rows else i
            return stats[2 * n : 2 * n + 1], stats[2 * n + 1 : 2 * n + 2]

        def tile(marks, queries, lanes, i, j):
            places = [(x, y) for x, y in around(i, j) if 0 <= x < rows and 0 <= y < cols]
            q = spread(queries.tile(0, i, j, 2), mask)
            g = spread(queries.tile(1, i, j, 2), mask)
            level, dot = stat_at(i, j, lanes)
            mark = marks.mark(mark_ref, i, j)
            keys = jnp.concatenate([marks.tile(0, x, y, 0) for x, y in places], axis=0)
            values = jnp.concatenate([marks.tile(1, x, y, 0) for x, y in places], axis=0)
            scores, grads = nt(keys, q), nt(values, g)
            yield
            probs, slopes = [], []
            for t, (x, y) in enumerate(places):
                less = jnp.where(mark * mark_ref[x, y].astype(F32) > 0, level, BIG)
                p = jnp.exp2(scores[rows_of(t)] * LOG2E - less)
                probs.append(p.astype(BF16))
                slopes.append((p * (grads[rows_of(t)] - dot)).astype(BF16))
            yield
            for n, (parts, right) in enumerate(((slopes, q), (probs, g))):
                part = nn(jnp.concatenate(parts, axis=0), right)
                for t, (x, y) in enumerate(places):
                    acc_ref[n, rows_of(x * cols + y), lanes] += part[rows_of(t)]

        def step(lanes):
            marks = Block(rows, cols, own_kv, near_kv, lanes)
            queries = Block(rows, cols, None, near_qg, lanes)
            outside = [
                (i, j) for i in range(-1, rows + 1) for j in range(-1, cols + 1)
                if not (0 <= i < rows and 0 <= j < cols)
            ]
            drive(tile(marks, queries, lanes, i, j) for i, j in outside)
            for x in range(rows):
                for y in range(cols):
                    put_tile(gk_ref, x, y, lanes, acc_ref[0, rows_of(x * cols + y), lanes])
                    put_tile(gv_ref, x, y, lanes, acc_ref[1, rows_of(x * cols + y), lanes])

        each_group(width, step)

    return body


def local(query_grid, key_grid, value_grid, out_grad, tissue):
    rows, cols = tissue.shape
    width = query_grid.shape[-1]
    own_kv, own_qg, (first_side, last_side) = pack((key_grid, value_grid, query_grid, out_grad), tissue)
    above_kv = shift(own_kv[-1], "rows", 1)
    below_kv = shift(own_kv[0], "rows", -1)
    grid_out = jax.ShapeDtypeStruct(query_grid.shape, BF16)
    stat_out = jax.ShapeDtypeStruct((2 * cols, width), F32)
    sum_out = jax.ShapeDtypeStruct((2, rows * cols * TOKENS, width), F32)
    part_out = jax.ShapeDtypeStruct((rows * cols * TOKENS, width), F32)
    level_out = jax.ShapeDtypeStruct((2 * rows * cols, width), F32)
    pairs = 9 * rows * cols * TOKENS * TOKENS * width
    part, level = call(
        forward_own(rows, cols, width), [part_out, level_out], (tissue, *own_kv, *own_qg),
        flops=8 * pairs, exps=pairs // (2 * HEAD),
    )
    first_side, last_side, *sent_qg, level = lax.optimization_barrier((first_side, last_side, own_qg[0], own_qg[-1], level))
    left = shift(last_side, "cols", 1)
    right = shift(first_side, "cols", -1)
    above_qg = shift(sent_qg[1], "rows", 1)
    below_qg = shift(sent_qg[0], "rows", -1)
    first_kv, last_kv = pack_corners(above_kv, below_kv, cols)
    near_kv = (above_kv, below_kv, left, right, shift(last_kv, "cols", 1), shift(first_kv, "cols", -1))
    attended, *stats = call(
        forward(rows, cols, width), [grid_out] + [stat_out] * rows,
        (tissue, *own_kv, *near_kv, *own_qg, part, level), flops=8 * pairs, exps=pairs // (2 * HEAD),
    )
    above_s = shift(stats[-1], "rows", 1)
    below_s = shift(stats[0], "rows", -1)
    query_parts = None
    for a in range(rows):
        args = (tissue, *own_kv, *near_kv, *own_qg, stats[a]) + (query_parts or ())
        query_parts = tuple(pl.pallas_call(
            backward(rows, cols, width, a),
            in_specs=[SMEM] + [VMEM] * (2 * rows + 7) + ([pl.BlockSpec(memory_space=pl.ANY), VMEM] if a else []),
            out_specs=[pl.BlockSpec(memory_space=pl.ANY), VMEM],
            out_shape=[grid_out, sum_out],
            scratch_shapes=[pltpu.VMEM((TILE,) + grid_out.shape[1:], BF16), pltpu.SemaphoreType.DMA],
            input_output_aliases={2 * rows + 8: 0} if a else {},
            compiler_params=pltpu.CompilerParams(vmem_limit_bytes=LIMIT),
            cost_estimate=pl.CostEstimate(flops=16 * pairs, transcendentals=pairs // (2 * HEAD), bytes_accessed=1 << 20),
        )(*args))
        if a == 0:
            above_s, below_s, sums = lax.optimization_barrier((above_s, below_s, query_parts[1]))
            query_parts = (query_parts[0], sums)
            first_q, last_q = pack_queries(stats, above_s, below_s, above_qg, below_qg, cols)
            near_qg = (above_qg, below_qg, left, right, shift(last_q, "cols", 1), shift(first_q, "cols", -1))
    grad_query, sums = query_parts
    args = (tissue, *own_kv, *near_kv, *near_qg, above_s, below_s, sums)
    grad_key, grad_value = pl.pallas_call(
        key_side(rows, cols, width),
        in_specs=[SMEM] + [VMEM] * (len(args) - 1),
        out_specs=[VMEM] * 2,
        out_shape=[grid_out] * 2,
        scratch_shapes=[pltpu.VMEM(sum_out.shape, F32)],
        compiler_params=pltpu.CompilerParams(vmem_limit_bytes=LIMIT),
        cost_estimate=pl.CostEstimate(flops=8 * pairs, transcendentals=pairs // (2 * HEAD), bytes_accessed=1 << 20),
    )(*args)
    return attended, grad_query, grad_key, grad_value


def solution(mesh):
    grid = P(("groups", "rows"), "cols", None)
    return jax.shard_map(
        local,
        mesh=mesh,
        in_specs=(grid, grid, grid, grid, P(("groups", "rows"), "cols")),
        out_specs=(grid, grid, grid, grid),
        check_vma=False,
    )
```

```python
import jax
import jax.numpy as jnp
from jax import lax
from jax.experimental import pallas as pl
from jax.experimental.pallas import tpu as pltpu
from jax.sharding import PartitionSpec as P

HEAD = 64
TILE = 8
TOKENS = TILE * TILE
LANES = 256
PER = LANES // HEAD
MARKS = 16
SCALE = HEAD ** -0.5
LOG2E = 1.4426950408889634
NEG = -1e30
BIG = 1e30
LIMIT = 20 * 1024 * 1024
VMEM = pl.BlockSpec(memory_space=pltpu.VMEM)
SMEM = pl.BlockSpec(memory_space=pltpu.SMEM)
BF16 = jnp.bfloat16
F32 = jnp.float32


def shift(array, axis, by):
    count = lax.axis_size(axis)
    pairs = [(i, i + by) for i in range(count) if 0 <= i + by < count]
    return lax.ppermute(array, axis, pairs)


def nt(a, b):
    return lax.dot_general(a, b, (((1,), (1,)), ((), ())), preferred_element_type=F32)


def nn(a, b):
    return lax.dot_general(a, b, (((1,), (0,)), ((), ())), preferred_element_type=F32)


def tn(a, b):
    return lax.dot_general(a, b, (((0,), (0,)), ((), ())), preferred_element_type=F32)


def call(body, out_shape, args, marks_first=True, flops=0, exps=0):
    size = sum(array.size * array.dtype.itemsize for array in args)
    return pl.pallas_call(
        body,
        in_specs=[SMEM if marks_first and n == 0 else VMEM for n in range(len(args))],
        out_specs=[VMEM] * len(out_shape),
        out_shape=out_shape,
        compiler_params=pltpu.CompilerParams(vmem_limit_bytes=LIMIT),
        cost_estimate=pl.CostEstimate(flops=flops, transcendentals=exps, bytes_accessed=size),
    )(*args)


def tile_of(ref, a, b):
    block = ref[TILE * a : TILE * (a + 1), TILE * b : TILE * (b + 1), :]
    return block.astype(F32).reshape(TOKENS, block.shape[-1])


def put_tile(ref, a, b, lanes, value):
    shaped = value.reshape(TILE, TILE, value.shape[-1]).astype(ref.dtype)
    ref[TILE * a : TILE * (a + 1), TILE * b : TILE * (b + 1), lanes] = shaped


def rows_of(index):
    return slice(index * TOKENS, (index + 1) * TOKENS)


def mark_row(ref, start, index, lanes):
    return ref[start : start + MARKS, lanes].astype(F32)[index : index + 1]


def write_marks(out, start, marks, width):
    which = lax.broadcasted_iota(jnp.int32, (MARKS, width), 0)
    rows = jnp.zeros((MARKS, width), F32)
    for n, mark in enumerate(marks):
        rows = jnp.where(which == n, mark, rows)
    out[start : start + MARKS, :] = rows.astype(BF16)


def pack(grids, tissue):
    rows, cols = tissue.shape
    width = grids[0].shape[-1]

    def body(mark_ref, *refs):
        sources, refs = refs[:4], refs[4:]
        kv_refs, qg_refs, side_refs = refs[:rows], refs[rows : 2 * rows], refs[2 * rows : 2 * rows + 2]
        grid_refs, sems = refs[2 * rows + 2 : 2 * rows + 6], refs[2 * rows + 6]

        copies = [
            [
                pltpu.make_async_copy(
                    source.at[TILE * a : TILE * (a + 1)], ref.at[TILE * a : TILE * (a + 1)], sems.at[n, a]
                )
                for a in range(rows)
            ]
            for n, (source, ref) in enumerate(zip(sources, grid_refs))
        ]
        for copy in sum(copies, []):
            copy.start()
        for n, ref in enumerate(grid_refs):
            for a in range(rows):
                copies[n][a].wait()
                out = (kv_refs if n < 2 else qg_refs)[a]
                for b in range(cols):
                    tile = tile_of(ref, a, b)
                    if n >= 2:
                        tile = tile * (SCALE if n == 2 else mark_ref[a, b].astype(F32))
                    tile = tile.astype(BF16)
                    out[rows_of(n % 2 * cols + b), :] = tile
                    for end, side in zip((0, cols - 1), side_refs):
                        if b == end:
                            side[rows_of(n * rows + a), :] = tile
        for a in range(rows):
            write_marks(kv_refs[a], 2 * cols * TOKENS, [mark_ref[a, b].astype(F32) for b in range(cols)], width)
        for b, side in zip((0, cols - 1), side_refs):
            write_marks(side, 4 * rows * TOKENS, [mark_ref[a, b].astype(F32) for a in range(rows)], width)

    shapes = [2 * cols * TOKENS + MARKS] * rows + [2 * cols * TOKENS] * rows + [4 * rows * TOKENS + MARKS] * 2
    shapes = [jax.ShapeDtypeStruct((height, width), BF16) for height in shapes]
    outs = pl.pallas_call(
        body,
        in_specs=[SMEM] + [pl.BlockSpec(memory_space=pltpu.HBM)] * 4,
        out_specs=[VMEM] * len(shapes),
        out_shape=shapes,
        scratch_shapes=[pltpu.VMEM(grid.shape, grid.dtype) for grid in grids] + [pltpu.SemaphoreType.DMA((4, rows))],
        compiler_params=pltpu.CompilerParams(vmem_limit_bytes=LIMIT),
        cost_estimate=pl.CostEstimate(flops=0, transcendentals=0, bytes_accessed=1 << 20),
    )(*(pltpu.with_memory_space_constraint(array, pltpu.HBM) for array in (tissue, *grids)))
    return outs[:rows], outs[rows : 2 * rows], outs[2 * rows :]


def pack_corners(above, below, cols):
    width = above.shape[1]

    def body(above_ref, below_ref, *outs):
        for b, out in zip((0, cols - 1), outs):
            for n in range(2):
                for end, ref in enumerate((above_ref, below_ref)):
                    out[rows_of(n * 2 + end), :] = ref[rows_of(n * cols + b), :]
            ends = [mark_row(ref, 2 * cols * TOKENS, b, slice(None)) for ref in (above_ref, below_ref)]
            write_marks(out, 4 * TOKENS, ends, width)

    shape = jax.ShapeDtypeStruct((4 * TOKENS + MARKS, width), BF16)
    return call(body, [shape] * 2, (above, below), marks_first=False)


def pieces(x):
    out = []
    for _ in range(3):
        out.append(x.astype(BF16))
        x = x - out[-1].astype(F32)
    return out


def pack_queries(stats, above_s, below_s, above_qg, below_qg, cols):
    rows = len(stats)
    width = above_s.shape[1]
    height = -(-6 * (rows + 2) // MARKS) * MARKS

    def body(*refs):
        stat_refs, ends, outs = refs[: rows + 2], refs[rows + 2 : rows + 4], refs[rows + 4 :]
        for b, out in zip((0, cols - 1), outs):
            for n in range(2):
                for end, ref in enumerate(ends):
                    out[rows_of(n * 2 + end), :] = ref[rows_of(n * cols + b), :]
            parts = pieces(jnp.concatenate([ref[2 * b : 2 * b + 2, :] for ref in stat_refs], axis=0))
            parts = [part.astype(F32) for part in parts]
            rest = height - 6 * (rows + 2)
            if rest:
                parts.append(jnp.zeros((rest, width), F32))
            out[4 * TOKENS :, :] = jnp.concatenate(parts, axis=0).astype(BF16)

    shape = jax.ShapeDtypeStruct((4 * TOKENS + height, width), BF16)
    return call(body, [shape] * 2, (*stats, above_s, below_s, above_qg, below_qg), marks_first=False)


def head_mask():
    row = lax.broadcasted_iota(jnp.int32, (LANES, LANES), 0) // HEAD
    lane = lax.broadcasted_iota(jnp.int32, (LANES, LANES), 1) // HEAD
    return row == lane


def spread(tile, mask):
    return jnp.where(mask, jnp.concatenate([tile] * PER, axis=0), jnp.zeros((), tile.dtype))


def gather_heads(full):
    lane = lax.broadcasted_iota(jnp.int32, (TOKENS, LANES), 1) // HEAD
    out = full[:TOKENS]
    for h in range(1, PER):
        out = jnp.where(lane == h, full[h * TOKENS : (h + 1) * TOKENS], out)
    return out


def fold(x, op):
    return op(x.reshape(x.shape[0] // 8, 8, x.shape[1]), axis=0)


class Block:
    def __init__(self, rows, cols, own, near, lanes):
        self.rows, self.cols, self.own, self.lanes = rows, cols, own, lanes
        self.above, self.below, self.left, self.right, self.corner_left, self.corner_right = near

    def tile(self, n, i, j, side):
        ends = {-1: (self.above, 0), self.rows: (self.below, 1)}
        if 0 <= j < self.cols:
            ref = ends[i][0] if i in ends else self.own[i]
            return ref[rows_of(n * self.cols + j), self.lanes]
        if i in ends:
            ref = self.corner_left if j < 0 else self.corner_right
            return ref[rows_of(n * 2 + ends[i][1]), self.lanes]
        ref = self.left if j < 0 else self.right
        return ref[rows_of((side + n) * self.rows + i), self.lanes]

    def mark(self, marks, i, j):
        ends = {-1: (self.above, 0), self.rows: (self.below, 1)}
        if 0 <= j < self.cols:
            if i not in ends:
                return marks[i, j].astype(F32)
            return mark_row(ends[i][0], 2 * self.cols * TOKENS, j, self.lanes)
        if i in ends:
            ref = self.corner_left if j < 0 else self.corner_right
            return mark_row(ref, 4 * TOKENS, ends[i][1], self.lanes)
        ref = self.left if j < 0 else self.right
        return mark_row(ref, 4 * self.rows * TOKENS, i, self.lanes)


WIDTH = 3


def drive(programs):
    active, waiting = [], list(programs)
    while active or waiting:
        active, waiting = active + waiting[:WIDTH], waiting[WIDTH:]
        active = [program for program in active if next(program, True) is None]


def around(a, b):
    return [(a + i, b + j) for j in (-1, 0, 1) for i in (-1, 0, 1)]


def each_group(width, programs):
    drive(sum((list(programs(pl.ds(g * LANES, LANES))) for g in range(width // LANES)), []))


def columns(first, second):
    rows = jnp.concatenate(
        [part.astype(F32) for row in (first, second) for part in pieces(row) + [jnp.zeros_like(row)] * 5], axis=0
    )
    index = lax.broadcasted_iota(jnp.int32, (MARKS, LANES), 0) // 8
    lane = lax.broadcasted_iota(jnp.int32, (MARKS, LANES), 1) // 128
    full = tn(rows.astype(BF16), jnp.where(index == lane, 1.0, 0.0).astype(BF16))
    return [
        gather_heads(jnp.concatenate([full[:, 128 * n : 128 * (n + 1)]] * (LANES // 128), axis=1)) for n in range(2)
    ]


def softmax_part(scores, allowed, top):
    for t, ok in enumerate(allowed):
        high = fold(scores[rows_of(t)], jnp.max)
        if ok is not None:
            high = jnp.where(ok, high, NEG)
        high = high * LOG2E
        top = high if top is None else jnp.maximum(top, high)
    return jnp.max(top, axis=0, keepdims=True)


def exponentials(scores, allowed, top):
    total = jnp.zeros((8, LANES), F32)
    low = []
    for t, ok in enumerate(allowed):
        less = top if ok is None else jnp.where(ok, top, BIG)
        e = jnp.exp2(scores[rows_of(t)] * LOG2E - less)
        total = total + fold(e, jnp.sum)
        low.append(e.astype(BF16))
    return jnp.concatenate(low, axis=0), jnp.sum(total, axis=0, keepdims=True)


def split_places(a, b, rows, cols):
    inside = [(i, j) for i, j in around(a, b) if 0 <= i < rows and 0 <= j < cols]
    return inside, [place for place in around(a, b) if place not in inside]


def forward_own(rows, cols, width):
    def body(mark_ref, *refs):
        own_kv, own_qg = refs[:rows], refs[rows : 2 * rows]
        part_ref, level_ref = refs[2 * rows :]
        mask = head_mask()

        def tile(block, lanes, a, b):
            places, _ = split_places(a, b, rows, cols)
            allowed = [None if place == (a, b) else mark_ref[a, b] * mark_ref[place] > 0 for place in places]
            q = spread(own_qg[a][rows_of(b), lanes], mask)
            scores = nt(jnp.concatenate([block.tile(0, i, j, 0) for i, j in places], axis=0), q)
            yield
            top = softmax_part(scores, allowed, None)
            yield
            low, total = exponentials(scores, allowed, top)
            yield
            full = tn(low, jnp.concatenate([block.tile(1, i, j, 0) for i, j in places], axis=0))
            yield
            index = a * cols + b
            part_ref[rows_of(index), lanes] = gather_heads(full)
            level_ref[2 * index : 2 * index + 1, lanes] = top
            level_ref[2 * index + 1 : 2 * index + 2, lanes] = total

        def step(lanes):
            block = Block(rows, cols, own_kv, (None,) * 6, lanes)
            return (tile(block, lanes, a, b) for a in range(rows) for b in range(cols))

        each_group(width, step)

    return body


def corner_places(a, b, rows, cols):
    return [(i, j) for i, j in around(a, b) if not 0 <= i < rows and not 0 <= j < cols]


def forward_near(rows, cols, width):
    def body(mark_ref, *refs):
        own_kv, near, own_qg = refs[:rows], refs[rows : rows + 4] + (None, None), refs[rows + 4 : 2 * rows + 4]
        part_ref, level_ref, part_out, level_out = refs[2 * rows + 4 :]
        mask = head_mask()

        def tile(block, lanes, a, b):
            _, places = split_places(a, b, rows, cols)
            places = [place for place in places if place not in corner_places(a, b, rows, cols)]
            index = a * cols + b
            first = level_ref[2 * index : 2 * index + 1, lanes]
            before = level_ref[2 * index + 1 : 2 * index + 2, lanes]
            if not places:
                part_out[rows_of(index), lanes] = part_ref[rows_of(index), lanes]
                level_out[2 * index : 2 * index + 2, lanes] = level_ref[2 * index : 2 * index + 2, lanes]
                return
            allowed = [mark_ref[a, b].astype(F32) * block.mark(mark_ref, *place) > 0 for place in places]
            q = spread(own_qg[a][rows_of(b), lanes], mask)
            scores = nt(jnp.concatenate([block.tile(0, i, j, 0) for i, j in places], axis=0), q)
            yield
            top = softmax_part(scores, allowed, jnp.broadcast_to(first, (8, LANES)))
            yield
            low, total = exponentials(scores, allowed, top)
            less = jnp.exp2(first - top)
            yield
            full = tn(low, jnp.concatenate([block.tile(1, i, j, 0) for i, j in places], axis=0))
            own_by, _ = columns(less, less)
            yield
            part_out[rows_of(index), lanes] = gather_heads(full) + part_ref[rows_of(index), lanes] * own_by
            level_out[2 * index : 2 * index + 1, lanes] = top
            level_out[2 * index + 1 : 2 * index + 2, lanes] = total + less * before

        def step(lanes):
            block = Block(rows, cols, own_kv, near, lanes)
            return (tile(block, lanes, a, b) for a in range(rows) for b in range(cols))

        each_group(width, step)

    return body


def forward_last(rows, cols, width):
    def body(mark_ref, *refs):
        near, own_qg = (None,) * 4 + tuple(refs[:2]), refs[2 : rows + 2]
        part_ref, level_ref, att_ref, *stat_refs = refs[rows + 2 :]
        mask = head_mask()

        def tile(block, lanes, a, b):
            places = corner_places(a, b, rows, cols)
            index = a * cols + b
            own_mark = mark_ref[a, b].astype(F32)
            top = level_ref[2 * index : 2 * index + 1, lanes]
            total = level_ref[2 * index + 1 : 2 * index + 2, lanes]
            if places:
                allowed = [own_mark * block.mark(mark_ref, *place) > 0 for place in places]
                q = spread(own_qg[a][rows_of(b), lanes], mask)
                scores = nt(jnp.concatenate([block.tile(0, i, j, 0) for i, j in places], axis=0), q)
                yield
                first, before = top, total
                top = softmax_part(scores, allowed, jnp.broadcast_to(first, (8, LANES)))
                yield
                low, total = exponentials(scores, allowed, top)
                less = jnp.exp2(first - top)
                total = total + less * before
                full = tn(low, jnp.concatenate([block.tile(1, i, j, 0) for i, j in places], axis=0))
                inverse = own_mark / total
                near_by, own_by = columns(inverse, inverse * less)
                yield
                att = gather_heads(full) * near_by + part_ref[rows_of(index), lanes] * own_by
            else:
                inverse = own_mark / total
                att = part_ref[rows_of(index), lanes] * columns(inverse, inverse)[0]
            att = att.astype(BF16).astype(F32)
            put_tile(att_ref, a, b, lanes, att)
            prod = (own_qg[a][rows_of(cols + b), lanes].astype(F32) * att).T
            dot = [jnp.sum(prod[rows_of(h)], axis=0, keepdims=True) for h in range(PER)]
            stat_refs[a][2 * b : 2 * b + 1, lanes] = top + jnp.log2(total)
            stat_refs[a][2 * b + 1 : 2 * b + 2, lanes] = jnp.concatenate(dot, axis=1)

        def step(lanes):
            block = Block(rows, cols, None, near, lanes)
            return (tile(block, lanes, a, b) for a in range(rows) for b in range(cols))

        each_group(width, step)

    return body


def backward(rows, cols, width, a):
    def body(mark_ref, *refs):
        own_kv, near, own_qg = refs[:rows], refs[rows : rows + 6], refs[rows + 6 : 2 * rows + 6]
        stat_ref, gone_ref, refs = refs[2 * rows + 6], refs[2 * rows + 7], refs[2 * rows + 8 :]
        gq_ref, sum_ref = refs[1 if a == 0 else 0], refs[2 if a == 0 else 1]
        mask = head_mask()
        if a == 0:
            copy = pltpu.make_async_copy(gone_ref, refs[0], refs[3])
            copy.start()
            sum_ref[...] = jnp.zeros(sum_ref.shape, F32)
        else:
            sum_ref[...] = gone_ref[...]

        def tile(block, lanes, b):
            places = around(a, b)
            own_mark = mark_ref[a, b].astype(F32)
            q = spread(own_qg[a][rows_of(b), lanes], mask)
            g = spread(own_qg[a][rows_of(cols + b), lanes], mask)
            keys = jnp.concatenate([block.tile(0, i, j, 0) for i, j in places], axis=0)
            values = jnp.concatenate([block.tile(1, i, j, 0) for i, j in places], axis=0)
            level = stat_ref[2 * b : 2 * b + 1, lanes]
            dot = stat_ref[2 * b + 1 : 2 * b + 2, lanes]
            scores, grads = nt(keys, q), nt(values, g)
            yield
            probs, slopes = [], []
            for t, place in enumerate(places):
                less = level
                if place != (a, b):
                    less = jnp.where(own_mark * block.mark(mark_ref, *place) > 0, level, BIG)
                p = jnp.exp2(scores[rows_of(t)] * LOG2E - less)
                probs.append(p.astype(BF16))
                slopes.append((p * (grads[rows_of(t)] - dot)).astype(BF16))
            yield
            gq = gather_heads(tn(jnp.concatenate(slopes, axis=0), keys)) * SCALE
            put_tile(gq_ref, 0, b, lanes, gq)
            inside = [t for t, (i, j) in enumerate(places) if 0 <= i < rows and 0 <= j < cols]
            for n, (parts, right) in enumerate(((slopes, q), (probs, g))):
                part = nn(jnp.concatenate([parts[t] for t in inside], axis=0), right)
                for u, t in enumerate(inside):
                    i, j = places[t]
                    sum_ref[n, rows_of(i * cols + j), lanes] += part[rows_of(u)]

        def step(lanes):
            block = Block(rows, cols, own_kv, near, lanes)
            return (tile(block, lanes, b) for b in range(cols))

        each_group(width, step)
        if a == 0:
            copy.wait()

    return body


def key_side(rows, cols, width, last):
    def body(mark_ref, *refs):
        own_kv, refs = refs[:rows], refs[rows:]
        if last:
            near_kv, near_qg, refs = (None, None, *refs[:4]), (None, None, *refs[4:8]), refs[8:]
            sum_ref, gq_parts, (gq_ref, *out_refs) = refs[0], refs[1 : rows + 1], refs[rows + 1 : rows + 4]
            acc_ref, *staged, sems = refs[rows + 4 :]
            moves = [
                pltpu.make_async_copy(part, gq_ref.at[TILE * a : TILE * (a + 1)], sems.at[a])
                for a, part in enumerate(gq_parts)
            ]
            for copy in moves:
                copy.start()
        else:
            near_kv, near_qg = (*refs[:2], *[None] * 4), (*refs[2:4], *[None] * 4)
            above_s, below_s, sum_ref, acc_ref = refs[4:]
        mask = head_mask()
        acc_ref[...] = sum_ref[...]

        def stat_at(i, j, lanes):
            if 0 <= j < cols:
                ref = above_s if i < 0 else below_s
                return ref[2 * j : 2 * j + 1, lanes], ref[2 * j + 1 : 2 * j + 2, lanes]
            ref = near_qg[4 if j < 0 else 5]
            parts = ref[4 * TOKENS :, lanes].astype(F32)
            count = 2 * (rows + 2)
            stats = parts[:count] + parts[count : 2 * count] + parts[2 * count : 3 * count]
            n = rows if i < 0 else rows + 1 if i >= rows else i
            return stats[2 * n : 2 * n + 1], stats[2 * n + 1 : 2 * n + 2]

        def tile(marks, queries, lanes, i, j):
            places = [(x, y) for x, y in around(i, j) if 0 <= x < rows and 0 <= y < cols]
            q = spread(queries.tile(0, i, j, 2), mask)
            g = spread(queries.tile(1, i, j, 2), mask)
            level, dot = stat_at(i, j, lanes)
            mark = marks.mark(mark_ref, i, j)
            keys = jnp.concatenate([marks.tile(0, x, y, 0) for x, y in places], axis=0)
            values = jnp.concatenate([marks.tile(1, x, y, 0) for x, y in places], axis=0)
            scores, grads = nt(keys, q), nt(values, g)
            yield
            probs, slopes = [], []
            for t, (x, y) in enumerate(places):
                less = jnp.where(mark * mark_ref[x, y].astype(F32) > 0, level, BIG)
                p = jnp.exp2(scores[rows_of(t)] * LOG2E - less)
                probs.append(p.astype(BF16))
                slopes.append((p * (grads[rows_of(t)] - dot)).astype(BF16))
            yield
            for n, (parts, right) in enumerate(((slopes, q), (probs, g))):
                part = nn(jnp.concatenate(parts, axis=0), right)
                for t, (x, y) in enumerate(places):
                    acc_ref[n, rows_of(x * cols + y), lanes] += part[rows_of(t)]

        def step(lanes):
            marks = Block(rows, cols, own_kv, near_kv, lanes)
            queries = Block(rows, cols, None, near_qg, lanes)
            outside = [
                (i, j) for i in range(-1, rows + 1) for j in range(-1, cols + 1)
                if (not 0 <= j < cols if last else 0 <= j < cols and not 0 <= i < rows)
            ]
            return (tile(marks, queries, lanes, i, j) for i, j in outside)

        each_group(width, step)
        if not last:
            return
        for g in range(width // LANES):
            lanes = pl.ds(g * LANES, LANES)
            for n in range(2):
                for x in range(rows):
                    for y in range(cols):
                        put_tile(staged[n], x, y, lanes, acc_ref[n, rows_of(x * cols + y), lanes])
                copy = pltpu.make_async_copy(
                    staged[n].at[:, :, lanes], out_refs[n].at[:, :, lanes], sems.at[rows + 2 * g + n]
                )
                copy.start()
                moves.append(copy)
        for copy in moves:
            copy.wait()

    return body


def local(query_grid, key_grid, value_grid, out_grad, tissue):
    rows, cols = tissue.shape
    width = query_grid.shape[-1]
    own_kv, own_qg, (first_side, last_side) = pack((key_grid, value_grid, query_grid, out_grad), tissue)
    above_kv = shift(own_kv[-1], "rows", 1)
    below_kv = shift(own_kv[0], "rows", -1)
    grid_out = jax.ShapeDtypeStruct(query_grid.shape, BF16)
    stat_out = jax.ShapeDtypeStruct((2 * cols, width), F32)
    sum_out = jax.ShapeDtypeStruct((2, rows * cols * TOKENS, width), F32)
    part_out = jax.ShapeDtypeStruct((rows * cols * TOKENS, width), F32)
    level_out = jax.ShapeDtypeStruct((2 * rows * cols, width), F32)
    pairs = 9 * rows * cols * TOKENS * TOKENS * width
    part, level = call(
        forward_own(rows, cols, width), [part_out, level_out], (tissue, *own_kv, *own_qg),
        flops=64 * pairs, exps=pairs // HEAD * 8,
    )
    *sent_qg, level = lax.optimization_barrier((own_qg[0], own_qg[-1], level))
    left = shift(last_side, "cols", 1)
    right = shift(first_side, "cols", -1)
    above_qg = shift(sent_qg[1], "rows", 1)
    below_qg = shift(sent_qg[0], "rows", -1)
    above_kv, below_kv, level = lax.optimization_barrier((above_kv, below_kv, level))
    first_kv, last_kv = pack_corners(above_kv, below_kv, cols)
    part, level = call(
        forward_near(rows, cols, width), [part_out, level_out],
        (tissue, *own_kv, above_kv, below_kv, left, right, *own_qg, part, level), flops=64 * pairs, exps=pairs // HEAD * 8,
    )
    corners_kv = (shift(last_kv, "cols", 1), shift(first_kv, "cols", -1))
    near_kv = (above_kv, below_kv, left, right, *corners_kv)
    attended, *stats = call(
        forward_last(rows, cols, width), [grid_out] + [stat_out] * rows,
        (tissue, *corners_kv, *own_qg, part, level), flops=4 * pairs, exps=pairs // (4 * HEAD),
    )
    above_s = shift(stats[-1], "rows", 1)
    below_s = shift(stats[0], "rows", -1)
    hbm = pl.BlockSpec(memory_space=pltpu.HBM)
    parts = []
    for a in range(rows):
        args = (tissue, *own_kv, *near_kv, *own_qg, stats[a], attended if a == 0 else sums)
        half_out = jax.ShapeDtypeStruct((TILE,) + grid_out.shape[1:], BF16)
        *done, part, sums = pl.pallas_call(
            backward(rows, cols, width, a),
            in_specs=[SMEM] + [VMEM] * (len(args) - 1),
            out_specs=[hbm] * (a == 0) + [VMEM, VMEM],
            out_shape=[grid_out] * (a == 0) + [half_out, sum_out],
            scratch_shapes=[pltpu.SemaphoreType.DMA] * (a == 0),
            compiler_params=pltpu.CompilerParams(vmem_limit_bytes=LIMIT),
            cost_estimate=pl.CostEstimate(flops=16 * pairs, transcendentals=pairs // (2 * HEAD), bytes_accessed=1 << 20),
        )(*args)
        parts.append(part)
        if a == 0:
            attended_out = done[0]
            above_s, below_s, sums = lax.optimization_barrier((above_s, below_s, sums))
            first_q, last_q = pack_queries(stats, above_s, below_s, above_qg, below_qg, cols)
            side_qg = (left, right, shift(last_q, "cols", 1), shift(first_q, "cols", -1))
    (sums,) = call(
        key_side(rows, cols, width, False), [sum_out],
        (tissue, *own_kv, above_kv, below_kv, above_qg, below_qg, above_s, below_s, sums),
        flops=8 * pairs, exps=pairs // (4 * HEAD),
    )
    args = (tissue, *own_kv, *near_kv[2:], *side_qg, sums, *parts)
    grad_query, grad_key, grad_value = pl.pallas_call(
        key_side(rows, cols, width, True),
        in_specs=[SMEM] + [VMEM] * (len(args) - 1),
        out_specs=[hbm] * 3,
        out_shape=[grid_out] * 3,
        scratch_shapes=[pltpu.VMEM(sum_out.shape, F32)] + [pltpu.VMEM(grid_out.shape, BF16)] * 2
        + [pltpu.SemaphoreType.DMA((rows + 2 * (width // LANES),))],
        compiler_params=pltpu.CompilerParams(vmem_limit_bytes=LIMIT),
        cost_estimate=pl.CostEstimate(flops=8 * pairs, transcendentals=pairs // (2 * HEAD), bytes_accessed=1 << 20),
    )(*args)
    return attended_out, grad_query, grad_key, grad_value


def solution(mesh):
    grid = P(("groups", "rows"), "cols", None)
    return jax.shard_map(
        local,
        mesh=mesh,
        in_specs=(grid, grid, grid, grid, P(("groups", "rows"), "cols")),
        out_specs=(grid, grid, grid, grid),
        check_vma=False,
    )
```

```python
import jax
import jax.numpy as jnp
from jax import lax
from jax.experimental import pallas as pl
from jax.experimental.pallas import tpu as pltpu
from jax.sharding import PartitionSpec as P

HEAD = 64
TILE = 8
TOKENS = TILE * TILE
LANES = 256
PER = LANES // HEAD
MARKS = 16
SCALE = HEAD ** -0.5
LOG2E = 1.4426950408889634
NEG = -1e30
BIG = 1e30
LIMIT = 20 * 1024 * 1024
VMEM = pl.BlockSpec(memory_space=pltpu.VMEM)
SMEM = pl.BlockSpec(memory_space=pltpu.SMEM)
BF16 = jnp.bfloat16
F32 = jnp.float32


def shift(array, axis, by):
    count = lax.axis_size(axis)
    pairs = [(i, i + by) for i in range(count) if 0 <= i + by < count]
    return lax.ppermute(array, axis, pairs)


def nt(a, b):
    return lax.dot_general(a, b, (((1,), (1,)), ((), ())), preferred_element_type=F32)


def nn(a, b):
    return lax.dot_general(a, b, (((1,), (0,)), ((), ())), preferred_element_type=F32)


def tn(a, b):
    return lax.dot_general(a, b, (((0,), (0,)), ((), ())), preferred_element_type=F32)


def call(body, out_shape, args, flops=0, exps=0):
    size = sum(array.size * array.dtype.itemsize for array in args)
    return pl.pallas_call(
        body,
        in_specs=[VMEM] * len(args),
        out_specs=[VMEM] * len(out_shape),
        out_shape=out_shape,
        compiler_params=pltpu.CompilerParams(vmem_limit_bytes=LIMIT),
        cost_estimate=pl.CostEstimate(flops=flops, transcendentals=exps, bytes_accessed=size),
    )(*args)


def tile_of(ref, a, b):
    block = ref[TILE * a : TILE * (a + 1), TILE * b : TILE * (b + 1), :]
    return block.astype(F32).reshape(TOKENS, block.shape[-1])


def put_tile(ref, a, b, lanes, value):
    shaped = value.reshape(TILE, TILE, value.shape[-1]).astype(ref.dtype)
    ref[TILE * a : TILE * (a + 1), TILE * b : TILE * (b + 1), lanes] = shaped


def rows_of(index):
    return slice(index * TOKENS, (index + 1) * TOKENS)


def mark_row(ref, start, index, lanes):
    return ref[start : start + MARKS, lanes].astype(F32)[index : index + 1]


def write_marks(out, start, marks, width):
    which = lax.broadcasted_iota(jnp.int32, (MARKS, width), 0)
    rows = jnp.zeros((MARKS, width), F32)
    for n, mark in enumerate(marks):
        rows = jnp.where(which == n, mark, rows)
    out[start : start + MARKS, :] = rows.astype(BF16)


def pack(grids, tissue):
    rows, cols = tissue.shape
    width = grids[0].shape[-1]

    def body(mark_ref, *refs):
        sources, refs = refs[:4], refs[4:]
        kv_refs, qg_refs, side_refs = refs[:rows], refs[rows : 2 * rows], refs[2 * rows : 2 * rows + 2]
        grid_refs, sems = refs[2 * rows + 2 : 2 * rows + 6], refs[2 * rows + 6]

        copies = [
            [
                pltpu.make_async_copy(
                    source.at[TILE * a : TILE * (a + 1)], ref.at[TILE * a : TILE * (a + 1)], sems.at[n, a]
                )
                for a in range(rows)
            ]
            for n, (source, ref) in enumerate(zip(sources, grid_refs))
        ]
        for copy in sum(copies, []):
            copy.start()
        for n, ref in enumerate(grid_refs):
            for a in range(rows):
                copies[n][a].wait()
                out = (kv_refs if n < 2 else qg_refs)[a]
                for b in range(cols):
                    tile = tile_of(ref, a, b)
                    if n >= 2:
                        tile = tile * (SCALE if n == 2 else mark_ref[a, b].astype(F32))
                    tile = tile.astype(BF16)
                    out[rows_of(n % 2 * cols + b), :] = tile
                    for end, side in zip((0, cols - 1), side_refs):
                        if b == end:
                            side[rows_of(n * rows + a), :] = tile
        for a in range(rows):
            write_marks(kv_refs[a], 2 * cols * TOKENS, [mark_ref[a, b].astype(F32) for b in range(cols)], width)
        for b, side in zip((0, cols - 1), side_refs):
            write_marks(side, 4 * rows * TOKENS, [mark_ref[a, b].astype(F32) for a in range(rows)], width)

    shapes = [2 * cols * TOKENS + MARKS] * rows + [2 * cols * TOKENS] * rows + [4 * rows * TOKENS + MARKS] * 2
    shapes = [jax.ShapeDtypeStruct((height, width), BF16) for height in shapes]
    outs = pl.pallas_call(
        body,
        in_specs=[SMEM] + [pl.BlockSpec(memory_space=pltpu.HBM)] * 4,
        out_specs=[VMEM] * len(shapes),
        out_shape=shapes,
        scratch_shapes=[pltpu.VMEM(grid.shape, grid.dtype) for grid in grids] + [pltpu.SemaphoreType.DMA((4, rows))],
        compiler_params=pltpu.CompilerParams(vmem_limit_bytes=LIMIT),
        cost_estimate=pl.CostEstimate(flops=0, transcendentals=0, bytes_accessed=1 << 20),
    )(*(pltpu.with_memory_space_constraint(array, pltpu.HBM) for array in (tissue, *grids)))
    return outs[:rows], outs[rows : 2 * rows], outs[2 * rows :]


def pack_corners(above, below, cols):
    width = above.shape[1]

    def body(above_ref, below_ref, *outs):
        for b, out in zip((0, cols - 1), outs):
            for n in range(2):
                for end, ref in enumerate((above_ref, below_ref)):
                    out[rows_of(n * 2 + end), :] = ref[rows_of(n * cols + b), :]
            ends = [mark_row(ref, 2 * cols * TOKENS, b, slice(None)) for ref in (above_ref, below_ref)]
            write_marks(out, 4 * TOKENS, ends, width)

    shape = jax.ShapeDtypeStruct((4 * TOKENS + MARKS, width), BF16)
    return call(body, [shape] * 2, (above, below))


def pieces(x):
    out = []
    for _ in range(3):
        out.append(x.astype(BF16))
        x = x - out[-1].astype(F32)
    return out


def pack_queries(stats, above_s, below_s, above_qg, below_qg, cols):
    rows = len(stats)
    width = above_s.shape[1]
    height = -(-6 * (rows + 2) // MARKS) * MARKS

    def body(*refs):
        stat_refs, ends, outs = refs[: rows + 2], refs[rows + 2 : rows + 4], refs[rows + 4 :]
        for b, out in zip((0, cols - 1), outs):
            for n in range(2):
                for end, ref in enumerate(ends):
                    out[rows_of(n * 2 + end), :] = ref[rows_of(n * cols + b), :]
            parts = pieces(jnp.concatenate([ref[2 * b : 2 * b + 2, :] for ref in stat_refs], axis=0))
            parts = [part.astype(F32) for part in parts]
            rest = height - 6 * (rows + 2)
            if rest:
                parts.append(jnp.zeros((rest, width), F32))
            out[4 * TOKENS :, :] = jnp.concatenate(parts, axis=0).astype(BF16)

    shape = jax.ShapeDtypeStruct((4 * TOKENS + height, width), BF16)
    return call(body, [shape] * 2, (*stats, above_s, below_s, above_qg, below_qg))


def head_mask():
    row = lax.broadcasted_iota(jnp.int32, (LANES, LANES), 0) // HEAD
    lane = lax.broadcasted_iota(jnp.int32, (LANES, LANES), 1) // HEAD
    return row == lane


def spread(tile, mask):
    return jnp.where(mask, jnp.concatenate([tile] * PER, axis=0), jnp.zeros((), tile.dtype))


def gather_heads(full):
    lane = lax.broadcasted_iota(jnp.int32, (TOKENS, LANES), 1) // HEAD
    out = full[:TOKENS]
    for h in range(1, PER):
        out = jnp.where(lane == h, full[h * TOKENS : (h + 1) * TOKENS], out)
    return out


def fold(x, op):
    return op(x.reshape(x.shape[0] // 8, 8, x.shape[1]), axis=0)


class Block:
    def __init__(self, rows, cols, own, near, lanes):
        self.rows, self.cols, self.own, self.lanes = rows, cols, own, lanes
        self.above, self.below, self.left, self.right, self.corner_left, self.corner_right = near

    def tile(self, n, i, j, side):
        ends = {-1: (self.above, 0), self.rows: (self.below, 1)}
        if 0 <= j < self.cols:
            ref = ends[i][0] if i in ends else self.own[i]
            return ref[rows_of(n * self.cols + j), self.lanes]
        if i in ends:
            ref = self.corner_left if j < 0 else self.corner_right
            return ref[rows_of(n * 2 + ends[i][1]), self.lanes]
        ref = self.left if j < 0 else self.right
        return ref[rows_of((side + n) * self.rows + i), self.lanes]

    def mark(self, i, j):
        ends = {-1: (self.above, 0), self.rows: (self.below, 1)}
        if 0 <= j < self.cols:
            if i not in ends:
                return mark_row(self.own[i], 2 * self.cols * TOKENS, j, self.lanes)
            return mark_row(ends[i][0], 2 * self.cols * TOKENS, j, self.lanes)
        if i in ends:
            ref = self.corner_left if j < 0 else self.corner_right
            return mark_row(ref, 4 * TOKENS, ends[i][1], self.lanes)
        ref = self.left if j < 0 else self.right
        return mark_row(ref, 4 * self.rows * TOKENS, i, self.lanes)


WIDTH = 3


def drive(programs):
    active, waiting = [], list(programs)
    while active or waiting:
        active, waiting = active + waiting[:WIDTH], waiting[WIDTH:]
        active = [program for program in active if next(program, True) is None]


def around(a, b):
    return [(a + i, b + j) for j in (-1, 0, 1) for i in (-1, 0, 1)]


def each_group(width, programs):
    drive(sum((list(programs(pl.ds(g * LANES, LANES))) for g in range(width // LANES)), []))


def columns(first, second):
    rows = jnp.concatenate(
        [part.astype(F32) for row in (first, second) for part in pieces(row) + [jnp.zeros_like(row)] * 5], axis=0
    )
    index = lax.broadcasted_iota(jnp.int32, (MARKS, LANES), 0) // 8
    lane = lax.broadcasted_iota(jnp.int32, (MARKS, LANES), 1) // 128
    full = tn(rows.astype(BF16), jnp.where(index == lane, 1.0, 0.0).astype(BF16))
    return [
        gather_heads(jnp.concatenate([full[:, 128 * n : 128 * (n + 1)]] * (LANES // 128), axis=1)) for n in range(2)
    ]


def softmax_part(scores, allowed, top):
    for t, ok in enumerate(allowed):
        high = fold(scores[rows_of(t)], jnp.max)
        if ok is not None:
            high = jnp.where(ok, high, NEG)
        high = high * LOG2E
        top = high if top is None else jnp.maximum(top, high)
    return jnp.max(top, axis=0, keepdims=True)


def exponentials(scores, allowed, top):
    total = jnp.zeros((8, LANES), F32)
    low = []
    for t, ok in enumerate(allowed):
        less = top if ok is None else jnp.where(ok, top, BIG)
        e = jnp.exp2(scores[rows_of(t)] * LOG2E - less)
        total = total + fold(e, jnp.sum)
        low.append(e.astype(BF16))
    return jnp.concatenate(low, axis=0), jnp.sum(total, axis=0, keepdims=True)


def split_places(a, b, rows, cols):
    inside = [(i, j) for i, j in around(a, b) if 0 <= i < rows and 0 <= j < cols]
    return inside, [place for place in around(a, b) if place not in inside]


def forward_own(rows, cols, width):
    def body(*refs):
        own_kv, own_qg = refs[:rows], refs[rows : 2 * rows]
        part_ref, level_ref = refs[2 * rows :]
        mask = head_mask()

        def tile(block, lanes, a, b):
            places, _ = split_places(a, b, rows, cols)
            allowed = [None if place == (a, b) else block.mark(a, b) * block.mark(*place) > 0 for place in places]
            q = spread(own_qg[a][rows_of(b), lanes], mask)
            scores = nt(jnp.concatenate([block.tile(0, i, j, 0) for i, j in places], axis=0), q)
            yield
            top = softmax_part(scores, allowed, None)
            yield
            low, total = exponentials(scores, allowed, top)
            yield
            full = tn(low, jnp.concatenate([block.tile(1, i, j, 0) for i, j in places], axis=0))
            yield
            index = a * cols + b
            part_ref[rows_of(index), lanes] = gather_heads(full)
            level_ref[2 * index : 2 * index + 1, lanes] = top
            level_ref[2 * index + 1 : 2 * index + 2, lanes] = total

        def step(lanes):
            block = Block(rows, cols, own_kv, (None,) * 6, lanes)
            return (tile(block, lanes, a, b) for a in range(rows) for b in range(cols))

        each_group(width, step)

    return body


def corner_places(a, b, rows, cols):
    return [(i, j) for i, j in around(a, b) if not 0 <= i < rows and not 0 <= j < cols]


def place(a, b):
    return slice(TILE * a, TILE * (a + 1)), slice(TILE * b, TILE * (b + 1))


def finish(att_ref, a, b, lanes, att, grads):
    att = att.astype(BF16).astype(F32)
    put_tile(att_ref, a, b, lanes, att)
    prod = (grads.astype(F32) * att).T
    return jnp.concatenate([jnp.sum(prod[rows_of(h)], axis=0, keepdims=True) for h in range(PER)], axis=1)


def forward_near(rows, cols, width):
    def body(*refs):
        own_kv, near, own_qg = refs[:rows], refs[rows : rows + 4] + (None, None), refs[rows + 4 : 2 * rows + 4]
        part_ref, level_ref, part_out, level_out, att_ref = refs[2 * rows + 4 :]
        mask = head_mask()

        def tile(block, lanes, a, b):
            _, places = split_places(a, b, rows, cols)
            places = [place for place in places if place not in corner_places(a, b, rows, cols)]
            index = a * cols + b
            first = level_ref[2 * index : 2 * index + 1, lanes]
            before = level_ref[2 * index + 1 : 2 * index + 2, lanes]
            allowed = [block.mark(a, b) * block.mark(*place) > 0 for place in places]
            q = spread(own_qg[a][rows_of(b), lanes], mask)
            scores = nt(jnp.concatenate([block.tile(0, i, j, 0) for i, j in places], axis=0), q)
            yield
            top = softmax_part(scores, allowed, jnp.broadcast_to(first, (8, LANES)))
            yield
            low, total = exponentials(scores, allowed, top)
            less = jnp.exp2(first - top)
            yield
            full = tn(low, jnp.concatenate([block.tile(1, i, j, 0) for i, j in places], axis=0))
            total = total + less * before
            if corner_places(a, b, rows, cols):
                own_by, _ = columns(less, less)
                yield
                part_out[rows_of(index), lanes] = gather_heads(full) + part_ref[rows_of(index), lanes] * own_by
                level_out[2 * index : 2 * index + 1, lanes] = top
                level_out[2 * index + 1 : 2 * index + 2, lanes] = total
                return
            inverse = block.mark(a, b) / total
            near_by, own_by = columns(inverse, inverse * less)
            yield
            att = gather_heads(full) * near_by + part_ref[rows_of(index), lanes] * own_by
            dot = finish(att_ref, a, b, lanes, att, own_qg[a][rows_of(cols + b), lanes])
            level_out[2 * index : 2 * index + 1, lanes] = top + jnp.log2(total)
            level_out[2 * index + 1 : 2 * index + 2, lanes] = dot

        def step(lanes):
            block = Block(rows, cols, own_kv, near, lanes)
            return (tile(block, lanes, a, b) for a in range(rows) for b in range(cols))

        each_group(width, step)

    return body


def forward_last(rows, cols, width):
    def body(*refs):
        own_kv, refs = refs[:rows], refs[rows:]
        near, own_qg = (None,) * 4 + tuple(refs[:2]), refs[2 : rows + 2]
        part_ref, level_ref, att_ref, *stat_refs = refs[rows + 2 :]
        mask = head_mask()

        def tile(block, lanes, a, b):
            places = corner_places(a, b, rows, cols)
            index = a * cols + b
            own_mark = block.mark(a, b)
            if not places:
                stat_refs[a][2 * b : 2 * b + 2, lanes] = level_ref[2 * index : 2 * index + 2, lanes]
                return
            first = level_ref[2 * index : 2 * index + 1, lanes]
            before = level_ref[2 * index + 1 : 2 * index + 2, lanes]
            allowed = [own_mark * block.mark(*place) > 0 for place in places]
            q = spread(own_qg[a][rows_of(b), lanes], mask)
            scores = nt(jnp.concatenate([block.tile(0, i, j, 0) for i, j in places], axis=0), q)
            yield
            top = softmax_part(scores, allowed, jnp.broadcast_to(first, (8, LANES)))
            yield
            low, total = exponentials(scores, allowed, top)
            less = jnp.exp2(first - top)
            total = total + less * before
            full = tn(low, jnp.concatenate([block.tile(1, i, j, 0) for i, j in places], axis=0))
            inverse = own_mark / total
            near_by, own_by = columns(inverse, inverse * less)
            yield
            att = gather_heads(full) * near_by + part_ref[rows_of(index), lanes] * own_by
            dot = finish(att_ref, a, b, lanes, att, own_qg[a][rows_of(cols + b), lanes])
            stat_refs[a][2 * b : 2 * b + 1, lanes] = top + jnp.log2(total)
            stat_refs[a][2 * b + 1 : 2 * b + 2, lanes] = dot

        def step(lanes):
            block = Block(rows, cols, own_kv, near, lanes)
            return (tile(block, lanes, a, b) for a in range(rows) for b in range(cols))

        each_group(width, step)

    return body


def backward(rows, cols, width, tiles, kind):
    def body(*refs):
        count = 4 if kind == 0 else 6
        own_kv, near, refs = refs[:rows], (*refs[rows : rows + count], None, None)[:6], refs[rows + count :]
        own_qg, stat_refs, refs = refs[:rows], refs[rows : 2 * rows], refs[2 * rows :]
        moves = []
        if kind == 0:
            gq_ref, sum_ref = refs
            sum_ref[...] = jnp.zeros(sum_ref.shape, F32)
        elif kind == 1:
            _, middle_ref, edge_ref, att_ref, gq_ref, sum_ref, sems = refs
            for a in range(rows):
                for b in range(cols):
                    source = edge_ref if corner_places(a, b, rows, cols) else middle_ref
                    where = place(a, b)
                    moves.append(pltpu.make_async_copy(source.at[where], att_ref.at[where], sems.at[a * cols + b]))
                    moves[-1].start()
        else:
            _, gq_ref, sum_ref = refs
        mask = head_mask()

        def tile(block, lanes, a, b):
            places = around(a, b)
            own_mark = block.mark(a, b)
            q = spread(own_qg[a][rows_of(b), lanes], mask)
            g = spread(own_qg[a][rows_of(cols + b), lanes], mask)
            keys = jnp.concatenate([block.tile(0, i, j, 0) for i, j in places], axis=0)
            values = jnp.concatenate([block.tile(1, i, j, 0) for i, j in places], axis=0)
            index = a * cols + b if kind == 0 else b
            level = stat_refs[a][2 * index : 2 * index + 1, lanes]
            dot = stat_refs[a][2 * index + 1 : 2 * index + 2, lanes]
            scores, grads = nt(keys, q), nt(values, g)
            yield
            probs, slopes = [], []
            for t, spot in enumerate(places):
                less = level
                if spot != (a, b):
                    less = jnp.where(own_mark * block.mark(*spot) > 0, level, BIG)
                p = jnp.exp2(scores[rows_of(t)] * LOG2E - less)
                probs.append(p.astype(BF16))
                slopes.append((p * (grads[rows_of(t)] - dot)).astype(BF16))
            yield
            gq = gather_heads(tn(jnp.concatenate(slopes, axis=0), keys)) * SCALE
            put_tile(gq_ref, a, b, lanes, gq)
            inside = [t for t, (i, j) in enumerate(places) if 0 <= i < rows and 0 <= j < cols]
            for n, (parts, right) in enumerate(((slopes, q), (probs, g))):
                part = nn(jnp.concatenate([parts[t] for t in inside], axis=0), right)
                for u, t in enumerate(inside):
                    i, j = places[t]
                    sum_ref[n, rows_of(i * cols + j), lanes] += part[rows_of(u)]

        def step(lanes):
            block = Block(rows, cols, own_kv, near, lanes)
            return (tile(block, lanes, a, b) for a, b in tiles)

        each_group(width, step)
        for copy in moves:
            copy.wait()

    return body


def key_side(rows, cols, width, last):
    def body(*refs):
        own_kv, refs = refs[:rows], refs[rows:]
        if last:
            near_kv, near_qg, refs = (None, None, *refs[:4]), (None, None, *refs[4:8]), refs[8:]
            middle, gq_parts = refs[1:3], refs[3 : rows + 4]
            gq_ref, *out_refs, acc_ref, staged_k, staged_v, sems = refs[rows + 4 :]
            staged = (staged_k, staged_v)
            moves = []

            def move(source, target):
                moves.append(pltpu.make_async_copy(source, target, sems.at[len(moves)]))
                moves[-1].start()

            for a in range(rows):
                for b in range(cols):
                    where = place(a, b)
                    move(gq_parts[a + 1 if corner_places(a, b, rows, cols) else 0].at[where], gq_ref.at[where])
            if cols > 2:
                where = slice(None), slice(TILE, TILE * (cols - 1))
                for n in range(2):
                    move(middle[n].at[where], out_refs[n].at[where])
        else:
            near_kv, near_qg = (*refs[:2], *[None] * 4), (*refs[2:4], *[None] * 4)
            above_s, below_s, _, acc_ref, *staged = refs[4:]
        mask = head_mask()

        def stat_at(i, j, lanes):
            if 0 <= j < cols:
                ref = above_s if i < 0 else below_s
                return ref[2 * j : 2 * j + 1, lanes], ref[2 * j + 1 : 2 * j + 2, lanes]
            ref = near_qg[4 if j < 0 else 5]
            parts = ref[4 * TOKENS :, lanes].astype(F32)
            count = 2 * (rows + 2)
            stats = parts[:count] + parts[count : 2 * count] + parts[2 * count : 3 * count]
            n = rows if i < 0 else rows + 1 if i >= rows else i
            return stats[2 * n : 2 * n + 1], stats[2 * n + 1 : 2 * n + 2]

        def tile(marks, queries, lanes, i, j):
            places = [(x, y) for x, y in around(i, j) if 0 <= x < rows and 0 <= y < cols]
            q = spread(queries.tile(0, i, j, 2), mask)
            g = spread(queries.tile(1, i, j, 2), mask)
            level, dot = stat_at(i, j, lanes)
            mark = marks.mark(i, j)
            keys = jnp.concatenate([marks.tile(0, x, y, 0) for x, y in places], axis=0)
            values = jnp.concatenate([marks.tile(1, x, y, 0) for x, y in places], axis=0)
            scores, grads = nt(keys, q), nt(values, g)
            yield
            probs, slopes = [], []
            for t, (x, y) in enumerate(places):
                less = jnp.where(mark * marks.mark(x, y) > 0, level, BIG)
                p = jnp.exp2(scores[rows_of(t)] * LOG2E - less)
                probs.append(p.astype(BF16))
                slopes.append((p * (grads[rows_of(t)] - dot)).astype(BF16))
            yield
            for n, (parts, right) in enumerate(((slopes, q), (probs, g))):
                part = nn(jnp.concatenate(parts, axis=0), right)
                for t, (x, y) in enumerate(places):
                    acc_ref[n, rows_of(x * cols + y), lanes] += part[rows_of(t)]

        def step(lanes):
            marks = Block(rows, cols, own_kv, near_kv, lanes)
            queries = Block(rows, cols, None, near_qg, lanes)
            outside = [
                (i, j) for i in range(-1, rows + 1) for j in range(-1, cols + 1)
                if (not 0 <= j < cols if last else 0 <= j < cols and not 0 <= i < rows)
            ]
            return (tile(marks, queries, lanes, i, j) for i, j in outside)

        each_group(width, step)
        done = (0, cols - 1) if last else range(1, cols - 1)
        done = sorted(set(done))
        for g in range(width // LANES):
            lanes = pl.ds(g * LANES, LANES)
            for n in range(2):
                for y in done:
                    for x in range(rows):
                        put_tile(staged[n], x, y, lanes, acc_ref[n, rows_of(x * cols + y), lanes])
                    if last:
                        where = slice(None), slice(TILE * y, TILE * (y + 1)), lanes
                        move(staged[n].at[where], out_refs[n].at[where])
        if not last:
            return
        for copy in moves:
            copy.wait()

    return body


def local(query_grid, key_grid, value_grid, out_grad, tissue):
    rows, cols = tissue.shape
    width = query_grid.shape[-1]
    own_kv, own_qg, (first_side, last_side) = pack((key_grid, value_grid, query_grid, out_grad), tissue)
    above_kv = shift(own_kv[-1], "rows", 1)
    below_kv = shift(own_kv[0], "rows", -1)
    grid_out = jax.ShapeDtypeStruct(query_grid.shape, BF16)
    stat_out = jax.ShapeDtypeStruct((2 * cols, width), F32)
    sum_out = jax.ShapeDtypeStruct((2, rows * cols * TOKENS, width), F32)
    part_out = jax.ShapeDtypeStruct((rows * cols * TOKENS, width), F32)
    level_out = jax.ShapeDtypeStruct((2 * rows * cols, width), F32)
    pairs = 9 * rows * cols * TOKENS * TOKENS * width
    part, level = call(
        forward_own(rows, cols, width), [part_out, level_out], (*own_kv, *own_qg),
        flops=64 * pairs, exps=pairs // HEAD * 8,
    )
    *sent_qg, level = lax.optimization_barrier((own_qg[0], own_qg[-1], level))
    left = shift(last_side, "cols", 1)
    right = shift(first_side, "cols", -1)
    above_qg = shift(sent_qg[1], "rows", 1)
    below_qg = shift(sent_qg[0], "rows", -1)
    above_kv, below_kv, level = lax.optimization_barrier((above_kv, below_kv, level))
    first_kv, last_kv = pack_corners(above_kv, below_kv, cols)
    part, level, middle = call(
        forward_near(rows, cols, width), [part_out, level_out, grid_out],
        (*own_kv, above_kv, below_kv, left, right, *own_qg, part, level), flops=64 * pairs, exps=pairs // HEAD * 8,
    )
    every = [(a, b) for a in range(rows) for b in range(cols)]
    hbm = pl.BlockSpec(memory_space=pltpu.HBM)

    def run(body, args, hbm_outs, vmem_outs, scratch, sums_at, sums_out, cost):
        return pl.pallas_call(
            body,
            in_specs=[VMEM] * len(args),
            out_specs=[hbm] * len(hbm_outs) + [VMEM] * len(vmem_outs),
            out_shape=hbm_outs + vmem_outs,
            scratch_shapes=scratch,
            input_output_aliases={} if sums_at is None else {sums_at: sums_out},
            compiler_params=pltpu.CompilerParams(vmem_limit_bytes=LIMIT),
            cost_estimate=pl.CostEstimate(flops=cost * pairs, transcendentals=cost * pairs // 32 // HEAD, bytes_accessed=1 << 20),
        )(*args)

    parts = []
    tiles = [spot for spot in every if not corner_places(*spot, rows, cols)]
    args = (*own_kv, above_kv, below_kv, left, right, *own_qg, *[level] * rows)
    part_gq, sums = run(backward(rows, cols, width, tiles, 0), args, [], [grid_out, sum_out], [], None, 1, 8)
    parts.append(part_gq)
    level, sums = lax.optimization_barrier((level, sums))
    corners_kv = (shift(last_kv, "cols", 1), shift(first_kv, "cols", -1))
    near_kv = (above_kv, below_kv, left, right, *corners_kv)
    edge, *stats = call(
        forward_last(rows, cols, width), [grid_out] + [stat_out] * rows,
        (*own_kv, *corners_kv, *own_qg, part, level), flops=4 * pairs, exps=pairs // (4 * HEAD),
    )
    above_s = shift(stats[-1], "rows", 1)
    below_s = shift(stats[0], "rows", -1)
    for a in range(rows):
        tiles = [spot for spot in every if spot[0] == a and corner_places(*spot, rows, cols)]
        args = (*own_kv, *near_kv, *own_qg, *stats, sums) + ((middle, edge) if a == 0 else ())
        *done, part_gq, sums = run(
            backward(rows, cols, width, tiles, 1 if a == 0 else 2), args, [grid_out] * (a == 0), [grid_out, sum_out],
            [pltpu.SemaphoreType.DMA((rows * cols,))] * (a == 0), 3 * rows + 6, 2 if a == 0 else 1, 16,
        )
        parts.append(part_gq)
        if a == 0:
            attended = done[0]
            above_s, below_s, sums = lax.optimization_barrier((above_s, below_s, sums))
            first_q, last_q = pack_queries(stats, above_s, below_s, above_qg, below_qg, cols)
            side_qg = (left, right, shift(last_q, "cols", 1), shift(first_q, "cols", -1))
    args = (*own_kv, above_kv, below_kv, above_qg, below_qg, above_s, below_s, sums)
    sums, *inner = run(key_side(rows, cols, width, False), args, [], [sum_out, grid_out, grid_out], [], rows + 6, 0, 8)
    args = (*own_kv, *near_kv[2:], *side_qg, sums, *inner, *parts)
    grad_query, grad_key, grad_value, _ = run(
        key_side(rows, cols, width, True), args, [grid_out] * 3, [sum_out],
        [pltpu.VMEM(grid_out.shape, BF16)] * 2 + [pltpu.SemaphoreType.DMA((rows * cols + 2 + 4 * (width // LANES),))],
        rows + 8, 3, 8,
    )
    return attended, grad_query, grad_key, grad_value


def solution(mesh):
    grid = P(("groups", "rows"), "cols", None)
    return jax.shard_map(
        local,
        mesh=mesh,
        in_specs=(grid, grid, grid, grid, P(("groups", "rows"), "cols")),
        out_specs=(grid, grid, grid, grid),
        check_vma=False,
    )
```

```python
import jax
import jax.numpy as jnp
from jax import lax
from jax.experimental import pallas as pl
from jax.experimental.pallas import tpu as pltpu
from jax.sharding import PartitionSpec as P

HEAD = 64
TILE = 8
TOKENS = TILE * TILE
LANES = 256
PER = LANES // HEAD
MARKS = 16
SCALE = HEAD ** -0.5
LOG2E = 1.4426950408889634
NEG = -1e30
BIG = 1e30
LIMIT = 20 * 1024 * 1024
VMEM = pl.BlockSpec(memory_space=pltpu.VMEM)
SMEM = pl.BlockSpec(memory_space=pltpu.SMEM)
BF16 = jnp.bfloat16
F32 = jnp.float32


def shift(array, axis, by):
    count = lax.axis_size(axis)
    pairs = [(i, i + by) for i in range(count) if 0 <= i + by < count]
    return lax.ppermute(array, axis, pairs)


def nt(a, b):
    return lax.dot_general(a, b, (((1,), (1,)), ((), ())), preferred_element_type=F32)


def nn(a, b):
    return lax.dot_general(a, b, (((1,), (0,)), ((), ())), preferred_element_type=F32)


def tn(a, b):
    return lax.dot_general(a, b, (((0,), (0,)), ((), ())), preferred_element_type=F32)


def call(body, out_shape, args, flops=0, exps=0):
    size = sum(array.size * array.dtype.itemsize for array in args)
    return pl.pallas_call(
        body,
        in_specs=[VMEM] * len(args),
        out_specs=[VMEM] * len(out_shape),
        out_shape=out_shape,
        compiler_params=pltpu.CompilerParams(vmem_limit_bytes=LIMIT),
        cost_estimate=pl.CostEstimate(flops=flops, transcendentals=exps, bytes_accessed=size),
    )(*args)


def tile_of(ref, a, b):
    block = ref[TILE * a : TILE * (a + 1), TILE * b : TILE * (b + 1), :]
    return block.astype(F32).reshape(TOKENS, block.shape[-1])


def put_tile(ref, a, b, lanes, value):
    shaped = value.reshape(TILE, TILE, value.shape[-1]).astype(ref.dtype)
    ref[TILE * a : TILE * (a + 1), TILE * b : TILE * (b + 1), lanes] = shaped


def rows_of(index):
    return slice(index * TOKENS, (index + 1) * TOKENS)


def mark_row(ref, start, index, lanes):
    return ref[start : start + MARKS, lanes].astype(F32)[index : index + 1]


def write_marks(out, start, marks, width):
    which = lax.broadcasted_iota(jnp.int32, (MARKS, width), 0)
    rows = jnp.zeros((MARKS, width), F32)
    for n, mark in enumerate(marks):
        rows = jnp.where(which == n, mark, rows)
    out[start : start + MARKS, :] = rows.astype(BF16)


def pack(grids, tissue):
    rows, cols = tissue.shape
    width = grids[0].shape[-1]

    def body(mark_hbm, *refs):
        sources, refs = refs[:4], refs[4:]
        kv_refs, qg_refs, side_refs = refs[:rows], refs[rows : 2 * rows], refs[2 * rows : 2 * rows + 2]
        grid_refs, (sems, mark_ref, mark_sem) = refs[2 * rows + 2 : 2 * rows + 6], refs[2 * rows + 6 :]

        copies = [
            [
                pltpu.make_async_copy(
                    source.at[TILE * a : TILE * (a + 1)], ref.at[TILE * a : TILE * (a + 1)], sems.at[n, a]
                )
                for a in range(rows)
            ]
            for n, (source, ref) in enumerate(zip(sources, grid_refs))
        ]
        for copy in sum(copies, []):
            copy.start()
        marks = pltpu.make_async_copy(mark_hbm, mark_ref, mark_sem)
        marks.start()
        marks.wait()
        for n, ref in enumerate(grid_refs):
            for a in range(rows):
                copies[n][a].wait()
                out = (kv_refs if n < 2 else qg_refs)[a]
                for b in range(cols):
                    tile = tile_of(ref, a, b)
                    if n >= 2:
                        tile = tile * (SCALE if n == 2 else mark_ref[a, b].astype(F32))
                    tile = tile.astype(BF16)
                    out[rows_of(n % 2 * cols + b), :] = tile
                    for end, side in zip((0, cols - 1), side_refs):
                        if b == end:
                            side[rows_of(n * rows + a), :] = tile
        for a in range(rows):
            write_marks(kv_refs[a], 2 * cols * TOKENS, [mark_ref[a, b].astype(F32) for b in range(cols)], width)
        for b, side in zip((0, cols - 1), side_refs):
            write_marks(side, 4 * rows * TOKENS, [mark_ref[a, b].astype(F32) for a in range(rows)], width)

    shapes = [2 * cols * TOKENS + MARKS] * rows + [2 * cols * TOKENS] * rows + [4 * rows * TOKENS + MARKS] * 2
    shapes = [jax.ShapeDtypeStruct((height, width), BF16) for height in shapes]
    outs = pl.pallas_call(
        body,
        in_specs=[pl.BlockSpec(memory_space=pltpu.HBM)] * 5,
        out_specs=[VMEM] * len(shapes),
        out_shape=shapes,
        scratch_shapes=[pltpu.VMEM(grid.shape, grid.dtype) for grid in grids] + [pltpu.SemaphoreType.DMA((4, rows))]
        + [pltpu.SMEM(tissue.shape, jnp.int32), pltpu.SemaphoreType.DMA],
        compiler_params=pltpu.CompilerParams(vmem_limit_bytes=LIMIT),
        cost_estimate=pl.CostEstimate(flops=0, transcendentals=0, bytes_accessed=1 << 20),
    )(*(pltpu.with_memory_space_constraint(array, pltpu.HBM) for array in (tissue, *grids)))
    return outs[:rows], outs[rows : 2 * rows], outs[2 * rows :]


def pack_corners(above, below, cols):
    width = above.shape[1]

    def body(above_ref, below_ref, *outs):
        for b, out in zip((0, cols - 1), outs):
            for n in range(2):
                for end, ref in enumerate((above_ref, below_ref)):
                    out[rows_of(n * 2 + end), :] = ref[rows_of(n * cols + b), :]
            ends = [mark_row(ref, 2 * cols * TOKENS, b, slice(None)) for ref in (above_ref, below_ref)]
            write_marks(out, 4 * TOKENS, ends, width)

    shape = jax.ShapeDtypeStruct((4 * TOKENS + MARKS, width), BF16)
    return call(body, [shape] * 2, (above, below))


def pieces(x):
    out = []
    for _ in range(3):
        out.append(x.astype(BF16))
        x = x - out[-1].astype(F32)
    return out


def pack_queries(stats, above_s, below_s, above_qg, below_qg, cols):
    rows = len(stats)
    width = above_s.shape[1]
    height = -(-6 * (rows + 2) // MARKS) * MARKS

    def body(*refs):
        stat_refs, ends, outs = refs[: rows + 2], refs[rows + 2 : rows + 4], refs[rows + 4 :]
        for b, out in zip((0, cols - 1), outs):
            for n in range(2):
                for end, ref in enumerate(ends):
                    out[rows_of(n * 2 + end), :] = ref[rows_of(n * cols + b), :]
            parts = pieces(jnp.concatenate([ref[2 * b : 2 * b + 2, :] for ref in stat_refs], axis=0))
            parts = [part.astype(F32) for part in parts]
            rest = height - 6 * (rows + 2)
            if rest:
                parts.append(jnp.zeros((rest, width), F32))
            out[4 * TOKENS :, :] = jnp.concatenate(parts, axis=0).astype(BF16)

    shape = jax.ShapeDtypeStruct((4 * TOKENS + height, width), BF16)
    return call(body, [shape] * 2, (*stats, above_s, below_s, above_qg, below_qg))


def head_mask():
    row = lax.broadcasted_iota(jnp.int32, (LANES, LANES), 0) // HEAD
    lane = lax.broadcasted_iota(jnp.int32, (LANES, LANES), 1) // HEAD
    return row == lane


def spread(tile, mask):
    return jnp.where(mask, jnp.concatenate([tile] * PER, axis=0), jnp.zeros((), tile.dtype))


def gather_heads(full):
    lane = lax.broadcasted_iota(jnp.int32, (TOKENS, LANES), 1) // HEAD
    out = full[:TOKENS]
    for h in range(1, PER):
        out = jnp.where(lane == h, full[h * TOKENS : (h + 1) * TOKENS], out)
    return out


def fold(x, op):
    return op(x.reshape(x.shape[0] // 8, 8, x.shape[1]), axis=0)


class Block:
    def __init__(self, rows, cols, own, near, lanes):
        self.rows, self.cols, self.own, self.lanes = rows, cols, own, lanes
        self.above, self.below, self.left, self.right, self.corner_left, self.corner_right = near

    def tile(self, n, i, j, side):
        ends = {-1: (self.above, 0), self.rows: (self.below, 1)}
        if 0 <= j < self.cols:
            ref = ends[i][0] if i in ends else self.own[i]
            return ref[rows_of(n * self.cols + j), self.lanes]
        if i in ends:
            ref = self.corner_left if j < 0 else self.corner_right
            return ref[rows_of(n * 2 + ends[i][1]), self.lanes]
        ref = self.left if j < 0 else self.right
        return ref[rows_of((side + n) * self.rows + i), self.lanes]

    def mark(self, i, j):
        ends = {-1: (self.above, 0), self.rows: (self.below, 1)}
        if 0 <= j < self.cols:
            if i not in ends:
                return mark_row(self.own[i], 2 * self.cols * TOKENS, j, self.lanes)
            return mark_row(ends[i][0], 2 * self.cols * TOKENS, j, self.lanes)
        if i in ends:
            ref = self.corner_left if j < 0 else self.corner_right
            return mark_row(ref, 4 * TOKENS, ends[i][1], self.lanes)
        ref = self.left if j < 0 else self.right
        return mark_row(ref, 4 * self.rows * TOKENS, i, self.lanes)


WIDTH = 3


def drive(programs):
    active, waiting = [], list(programs)
    while active or waiting:
        active, waiting = active + waiting[:WIDTH], waiting[WIDTH:]
        active = [program for program in active if next(program, True) is None]


def around(a, b):
    return [(a + i, b + j) for j in (-1, 0, 1) for i in (-1, 0, 1)]


def each_group(width, programs):
    drive(sum((list(programs(pl.ds(g * LANES, LANES))) for g in range(width // LANES)), []))


def columns(first, second):
    rows = jnp.concatenate(
        [part.astype(F32) for row in (first, second) for part in pieces(row) + [jnp.zeros_like(row)] * 5], axis=0
    )
    index = lax.broadcasted_iota(jnp.int32, (MARKS, LANES), 0) // 8
    lane = lax.broadcasted_iota(jnp.int32, (MARKS, LANES), 1) // 128
    full = tn(rows.astype(BF16), jnp.where(index == lane, 1.0, 0.0).astype(BF16))
    return [
        gather_heads(jnp.concatenate([full[:, 128 * n : 128 * (n + 1)]] * (LANES // 128), axis=1)) for n in range(2)
    ]


def softmax_part(scores, allowed, top):
    for t, ok in enumerate(allowed):
        high = fold(scores[rows_of(t)], jnp.max)
        if ok is not None:
            high = jnp.where(ok, high, NEG)
        high = high * LOG2E
        top = high if top is None else jnp.maximum(top, high)
    return jnp.max(top, axis=0, keepdims=True)


def exponentials(scores, allowed, top):
    total = jnp.zeros((8, LANES), F32)
    low = []
    for t, ok in enumerate(allowed):
        less = top if ok is None else jnp.where(ok, top, BIG)
        e = jnp.exp2(scores[rows_of(t)] * LOG2E - less)
        total = total + fold(e, jnp.sum)
        low.append(e.astype(BF16))
    return jnp.concatenate(low, axis=0), jnp.sum(total, axis=0, keepdims=True)


def split_places(a, b, rows, cols):
    inside = [(i, j) for i, j in around(a, b) if 0 <= i < rows and 0 <= j < cols]
    return inside, [place for place in around(a, b) if place not in inside]


def forward_own(rows, cols, width):
    def body(*refs):
        own_kv, own_qg = refs[:rows], refs[rows : 2 * rows]
        part_ref, level_ref = refs[2 * rows :]
        mask = head_mask()

        def tile(block, lanes, a, b):
            places, _ = split_places(a, b, rows, cols)
            allowed = [None if place == (a, b) else block.mark(a, b) * block.mark(*place) > 0 for place in places]
            q = spread(own_qg[a][rows_of(b), lanes], mask)
            scores = nt(jnp.concatenate([block.tile(0, i, j, 0) for i, j in places], axis=0), q)
            yield
            top = softmax_part(scores, allowed, None)
            yield
            low, total = exponentials(scores, allowed, top)
            yield
            full = tn(low, jnp.concatenate([block.tile(1, i, j, 0) for i, j in places], axis=0))
            yield
            index = a * cols + b
            part_ref[rows_of(index), lanes] = gather_heads(full)
            level_ref[2 * index : 2 * index + 1, lanes] = top
            level_ref[2 * index + 1 : 2 * index + 2, lanes] = total

        def step(lanes):
            block = Block(rows, cols, own_kv, (None,) * 6, lanes)
            return (tile(block, lanes, a, b) for a in range(rows) for b in range(cols))

        each_group(width, step)

    return body


def corner_places(a, b, rows, cols):
    return [(i, j) for i, j in around(a, b) if not 0 <= i < rows and not 0 <= j < cols]


def place(a, b):
    return slice(TILE * a, TILE * (a + 1)), slice(TILE * b, TILE * (b + 1))


def finish(att_ref, a, b, lanes, att, grads):
    att = att.astype(BF16).astype(F32)
    put_tile(att_ref, a, b, lanes, att)
    prod = (grads.astype(F32) * att).T
    return jnp.concatenate([jnp.sum(prod[rows_of(h)], axis=0, keepdims=True) for h in range(PER)], axis=1)


def forward_near(rows, cols, width):
    def body(*refs):
        own_kv, near, own_qg = refs[:rows], refs[rows : rows + 4] + (None, None), refs[rows + 4 : 2 * rows + 4]
        part_ref, level_ref, part_out, level_out, att_ref = refs[2 * rows + 4 :]
        mask = head_mask()

        def tile(block, lanes, a, b):
            _, places = split_places(a, b, rows, cols)
            places = [place for place in places if place not in corner_places(a, b, rows, cols)]
            index = a * cols + b
            first = level_ref[2 * index : 2 * index + 1, lanes]
            before = level_ref[2 * index + 1 : 2 * index + 2, lanes]
            allowed = [block.mark(a, b) * block.mark(*place) > 0 for place in places]
            q = spread(own_qg[a][rows_of(b), lanes], mask)
            scores = nt(jnp.concatenate([block.tile(0, i, j, 0) for i, j in places], axis=0), q)
            yield
            top = softmax_part(scores, allowed, jnp.broadcast_to(first, (8, LANES)))
            yield
            low, total = exponentials(scores, allowed, top)
            less = jnp.exp2(first - top)
            yield
            full = tn(low, jnp.concatenate([block.tile(1, i, j, 0) for i, j in places], axis=0))
            total = total + less * before
            if corner_places(a, b, rows, cols):
                own_by, _ = columns(less, less)
                yield
                part_out[rows_of(index), lanes] = gather_heads(full) + part_ref[rows_of(index), lanes] * own_by
                level_out[2 * index : 2 * index + 1, lanes] = top
                level_out[2 * index + 1 : 2 * index + 2, lanes] = total
                return
            inverse = block.mark(a, b) / total
            near_by, own_by = columns(inverse, inverse * less)
            yield
            att = gather_heads(full) * near_by + part_ref[rows_of(index), lanes] * own_by
            dot = finish(att_ref, a, b, lanes, att, own_qg[a][rows_of(cols + b), lanes])
            level_out[2 * index : 2 * index + 1, lanes] = top + jnp.log2(total)
            level_out[2 * index + 1 : 2 * index + 2, lanes] = dot

        def step(lanes):
            block = Block(rows, cols, own_kv, near, lanes)
            return (tile(block, lanes, a, b) for a in range(rows) for b in range(cols))

        each_group(width, step)

    return body


def forward_last(rows, cols, width):
    def body(*refs):
        own_kv, refs = refs[:rows], refs[rows:]
        near, own_qg = (None,) * 4 + tuple(refs[:2]), refs[2 : rows + 2]
        part_ref, level_ref, att_ref, *stat_refs = refs[rows + 2 :]
        mask = head_mask()

        def tile(block, lanes, a, b):
            places = corner_places(a, b, rows, cols)
            index = a * cols + b
            own_mark = block.mark(a, b)
            if not places:
                stat_refs[a][2 * b : 2 * b + 2, lanes] = level_ref[2 * index : 2 * index + 2, lanes]
                return
            first = level_ref[2 * index : 2 * index + 1, lanes]
            before = level_ref[2 * index + 1 : 2 * index + 2, lanes]
            allowed = [own_mark * block.mark(*place) > 0 for place in places]
            q = spread(own_qg[a][rows_of(b), lanes], mask)
            scores = nt(jnp.concatenate([block.tile(0, i, j, 0) for i, j in places], axis=0), q)
            yield
            top = softmax_part(scores, allowed, jnp.broadcast_to(first, (8, LANES)))
            yield
            low, total = exponentials(scores, allowed, top)
            less = jnp.exp2(first - top)
            total = total + less * before
            full = tn(low, jnp.concatenate([block.tile(1, i, j, 0) for i, j in places], axis=0))
            inverse = own_mark / total
            near_by, own_by = columns(inverse, inverse * less)
            yield
            att = gather_heads(full) * near_by + part_ref[rows_of(index), lanes] * own_by
            dot = finish(att_ref, a, b, lanes, att, own_qg[a][rows_of(cols + b), lanes])
            stat_refs[a][2 * b : 2 * b + 1, lanes] = top + jnp.log2(total)
            stat_refs[a][2 * b + 1 : 2 * b + 2, lanes] = dot

        def step(lanes):
            block = Block(rows, cols, own_kv, near, lanes)
            return (tile(block, lanes, a, b) for a in range(rows) for b in range(cols))

        each_group(width, step)

    return body


def backward(rows, cols, width, tiles, kind):
    def body(*refs):
        count = 4 if kind == 0 else 6
        own_kv, near, refs = refs[:rows], (*refs[rows : rows + count], None, None)[:6], refs[rows + count :]
        own_qg, stat_refs, refs = refs[:rows], refs[rows : 2 * rows], refs[2 * rows :]
        moves = []
        if kind == 0:
            gq_ref, sum_ref = refs
            sum_ref[...] = jnp.zeros(sum_ref.shape, F32)
        elif kind == 1:
            _, middle_ref, edge_ref, att_ref, gq_ref, sum_ref, sems = refs
            for a in range(rows):
                for b in range(cols):
                    source = edge_ref if corner_places(a, b, rows, cols) else middle_ref
                    where = place(a, b)
                    moves.append(pltpu.make_async_copy(source.at[where], att_ref.at[where], sems.at[a * cols + b]))
                    moves[-1].start()
        else:
            _, gq_ref, sum_ref = refs
        mask = head_mask()

        def tile(block, lanes, a, b):
            places = around(a, b)
            own_mark = block.mark(a, b)
            q = spread(own_qg[a][rows_of(b), lanes], mask)
            g = spread(own_qg[a][rows_of(cols + b), lanes], mask)
            keys = jnp.concatenate([block.tile(0, i, j, 0) for i, j in places], axis=0)
            values = jnp.concatenate([block.tile(1, i, j, 0) for i, j in places], axis=0)
            index = a * cols + b if kind == 0 else b
            level = stat_refs[a][2 * index : 2 * index + 1, lanes]
            dot = stat_refs[a][2 * index + 1 : 2 * index + 2, lanes]
            scores, grads = nt(keys, q), nt(values, g)
            yield
            probs, slopes = [], []
            for t, spot in enumerate(places):
                less = level
                if spot != (a, b):
                    less = jnp.where(own_mark * block.mark(*spot) > 0, level, BIG)
                p = jnp.exp2(scores[rows_of(t)] * LOG2E - less)
                probs.append(p.astype(BF16))
                slopes.append((p * (grads[rows_of(t)] - dot)).astype(BF16))
            yield
            gq = gather_heads(tn(jnp.concatenate(slopes, axis=0), keys)) * SCALE
            put_tile(gq_ref, a, b, lanes, gq)
            inside = [t for t, (i, j) in enumerate(places) if 0 <= i < rows and 0 <= j < cols]
            for n, (parts, right) in enumerate(((slopes, q), (probs, g))):
                part = nn(jnp.concatenate([parts[t] for t in inside], axis=0), right)
                for u, t in enumerate(inside):
                    i, j = places[t]
                    sum_ref[n, rows_of(i * cols + j), lanes] += part[rows_of(u)]

        def step(lanes):
            block = Block(rows, cols, own_kv, near, lanes)
            return (tile(block, lanes, a, b) for a, b in tiles)

        each_group(width, step)
        for copy in moves:
            copy.wait()

    return body


def key_side(rows, cols, width, last):
    def body(*refs):
        own_kv, refs = refs[:rows], refs[rows:]
        if last:
            near_kv, near_qg, refs = (None, None, *refs[:4]), (None, None, *refs[4:8]), refs[8:]
            middle, gq_parts = refs[1:3], refs[3 : rows + 4]
            gq_ref, *out_refs, acc_ref, staged_k, staged_v, sems = refs[rows + 4 :]
            staged = (staged_k, staged_v)
            moves = []

            def move(source, target):
                moves.append(pltpu.make_async_copy(source, target, sems.at[len(moves)]))
                moves[-1].start()

            for a in range(rows):
                for b in range(cols):
                    where = place(a, b)
                    move(gq_parts[a + 1 if corner_places(a, b, rows, cols) else 0].at[where], gq_ref.at[where])
            if cols > 2:
                where = slice(None), slice(TILE, TILE * (cols - 1))
                for n in range(2):
                    move(middle[n].at[where], out_refs[n].at[where])
        else:
            near_kv, near_qg = (*refs[:2], *[None] * 4), (*refs[2:4], *[None] * 4)
            above_s, below_s, _, acc_ref, *staged = refs[4:]
        mask = head_mask()

        def stat_at(i, j, lanes):
            if 0 <= j < cols:
                ref = above_s if i < 0 else below_s
                return ref[2 * j : 2 * j + 1, lanes], ref[2 * j + 1 : 2 * j + 2, lanes]
            ref = near_qg[4 if j < 0 else 5]
            parts = ref[4 * TOKENS :, lanes].astype(F32)
            count = 2 * (rows + 2)
            stats = parts[:count] + parts[count : 2 * count] + parts[2 * count : 3 * count]
            n = rows if i < 0 else rows + 1 if i >= rows else i
            return stats[2 * n : 2 * n + 1], stats[2 * n + 1 : 2 * n + 2]

        def tile(marks, queries, lanes, i, j):
            places = [(x, y) for x, y in around(i, j) if 0 <= x < rows and 0 <= y < cols]
            q = spread(queries.tile(0, i, j, 2), mask)
            g = spread(queries.tile(1, i, j, 2), mask)
            level, dot = stat_at(i, j, lanes)
            mark = marks.mark(i, j)
            keys = jnp.concatenate([marks.tile(0, x, y, 0) for x, y in places], axis=0)
            values = jnp.concatenate([marks.tile(1, x, y, 0) for x, y in places], axis=0)
            scores, grads = nt(keys, q), nt(values, g)
            yield
            probs, slopes = [], []
            for t, (x, y) in enumerate(places):
                less = jnp.where(mark * marks.mark(x, y) > 0, level, BIG)
                p = jnp.exp2(scores[rows_of(t)] * LOG2E - less)
                probs.append(p.astype(BF16))
                slopes.append((p * (grads[rows_of(t)] - dot)).astype(BF16))
            yield
            for n, (parts, right) in enumerate(((slopes, q), (probs, g))):
                part = nn(jnp.concatenate(parts, axis=0), right)
                for t, (x, y) in enumerate(places):
                    acc_ref[n, rows_of(x * cols + y), lanes] += part[rows_of(t)]

        def step(lanes):
            marks = Block(rows, cols, own_kv, near_kv, lanes)
            queries = Block(rows, cols, None, near_qg, lanes)
            outside = [
                (i, j) for i in range(-1, rows + 1) for j in range(-1, cols + 1)
                if (not 0 <= j < cols if last else 0 <= j < cols and not 0 <= i < rows)
            ]
            return (tile(marks, queries, lanes, i, j) for i, j in outside)

        each_group(width, step)
        done = (0, cols - 1) if last else range(1, cols - 1)
        done = sorted(set(done))
        for g in range(width // LANES):
            lanes = pl.ds(g * LANES, LANES)
            for n in range(2):
                for y in done:
                    for x in range(rows):
                        put_tile(staged[n], x, y, lanes, acc_ref[n, rows_of(x * cols + y), lanes])
                    if last:
                        where = slice(None), slice(TILE * y, TILE * (y + 1)), lanes
                        move(staged[n].at[where], out_refs[n].at[where])
        if not last:
            return
        for copy in moves:
            copy.wait()

    return body


def local(query_grid, key_grid, value_grid, out_grad, tissue):
    rows, cols = tissue.shape
    width = query_grid.shape[-1]
    own_kv, own_qg, (first_side, last_side) = pack((key_grid, value_grid, query_grid, out_grad), tissue)
    above_kv = shift(own_kv[-1], "rows", 1)
    below_kv = shift(own_kv[0], "rows", -1)
    grid_out = jax.ShapeDtypeStruct(query_grid.shape, BF16)
    stat_out = jax.ShapeDtypeStruct((2 * cols, width), F32)
    sum_out = jax.ShapeDtypeStruct((2, rows * cols * TOKENS, width), F32)
    part_out = jax.ShapeDtypeStruct((rows * cols * TOKENS, width), F32)
    level_out = jax.ShapeDtypeStruct((2 * rows * cols, width), F32)
    pairs = 9 * rows * cols * TOKENS * TOKENS * width
    part, level = call(
        forward_own(rows, cols, width), [part_out, level_out], (*own_kv, *own_qg),
        flops=64 * pairs, exps=pairs // HEAD * 8,
    )
    *sent_qg, level = lax.optimization_barrier((own_qg[0], own_qg[-1], level))
    left = shift(last_side, "cols", 1)
    right = shift(first_side, "cols", -1)
    above_qg = shift(sent_qg[1], "rows", 1)
    below_qg = shift(sent_qg[0], "rows", -1)
    above_kv, below_kv, level = lax.optimization_barrier((above_kv, below_kv, level))
    first_kv, last_kv = pack_corners(above_kv, below_kv, cols)
    part, level, middle = call(
        forward_near(rows, cols, width), [part_out, level_out, grid_out],
        (*own_kv, above_kv, below_kv, left, right, *own_qg, part, level), flops=64 * pairs, exps=pairs // HEAD * 8,
    )
    every = [(a, b) for a in range(rows) for b in range(cols)]
    hbm = pl.BlockSpec(memory_space=pltpu.HBM)

    def run(body, args, hbm_outs, vmem_outs, scratch, sums_at, sums_out, cost):
        return pl.pallas_call(
            body,
            in_specs=[VMEM] * len(args),
            out_specs=[hbm] * len(hbm_outs) + [VMEM] * len(vmem_outs),
            out_shape=hbm_outs + vmem_outs,
            scratch_shapes=scratch,
            input_output_aliases={} if sums_at is None else {sums_at: sums_out},
            compiler_params=pltpu.CompilerParams(vmem_limit_bytes=LIMIT),
            cost_estimate=pl.CostEstimate(flops=cost * pairs, transcendentals=cost * pairs // 32 // HEAD, bytes_accessed=1 << 20),
        )(*args)

    parts = []
    tiles = [spot for spot in every if not corner_places(*spot, rows, cols)]
    args = (*own_kv, above_kv, below_kv, left, right, *own_qg, *[level] * rows)
    part_gq, sums = run(backward(rows, cols, width, tiles, 0), args, [], [grid_out, sum_out], [], None, 1, 8)
    parts.append(part_gq)
    level, sums = lax.optimization_barrier((level, sums))
    corners_kv = (shift(last_kv, "cols", 1), shift(first_kv, "cols", -1))
    near_kv = (above_kv, below_kv, left, right, *corners_kv)
    edge, *stats = call(
        forward_last(rows, cols, width), [grid_out] + [stat_out] * rows,
        (*own_kv, *corners_kv, *own_qg, part, level), flops=4 * pairs, exps=pairs // (4 * HEAD),
    )
    above_s = shift(stats[-1], "rows", 1)
    below_s = shift(stats[0], "rows", -1)
    for a in range(rows):
        tiles = [spot for spot in every if spot[0] == a and corner_places(*spot, rows, cols)]
        args = (*own_kv, *near_kv, *own_qg, *stats, sums) + ((middle, edge) if a == 0 else ())
        *done, part_gq, sums = run(
            backward(rows, cols, width, tiles, 1 if a == 0 else 2), args, [grid_out] * (a == 0), [grid_out, sum_out],
            [pltpu.SemaphoreType.DMA((rows * cols,))] * (a == 0), 3 * rows + 6, 2 if a == 0 else 1, 16,
        )
        parts.append(part_gq)
        if a == 0:
            attended = done[0]
            above_s, below_s, sums = lax.optimization_barrier((above_s, below_s, sums))
            first_q, last_q = pack_queries(stats, above_s, below_s, above_qg, below_qg, cols)
            side_qg = (left, right, shift(last_q, "cols", 1), shift(first_q, "cols", -1))
    args = (*own_kv, above_kv, below_kv, above_qg, below_qg, above_s, below_s, sums)
    sums, *inner = run(key_side(rows, cols, width, False), args, [], [sum_out, grid_out, grid_out], [], rows + 6, 0, 8)
    args = (*own_kv, *near_kv[2:], *side_qg, sums, *inner, *parts)
    grad_query, grad_key, grad_value, _ = run(
        key_side(rows, cols, width, True), args, [grid_out] * 3, [sum_out],
        [pltpu.VMEM(grid_out.shape, BF16)] * 2 + [pltpu.SemaphoreType.DMA((rows * cols + 2 + 4 * (width // LANES),))],
        rows + 8, 3, 8,
    )
    return attended, grad_query, grad_key, grad_value


def solution(mesh):
    grid = P(("groups", "rows"), "cols", None)
    return jax.shard_map(
        local,
        mesh=mesh,
        in_specs=(grid, grid, grid, grid, P(("groups", "rows"), "cols")),
        out_specs=(grid, grid, grid, grid),
        check_vma=False,
    )
```

```python
import jax
import jax.numpy as jnp
from jax import lax
from jax.experimental import pallas as pl
from jax.experimental.pallas import tpu as pltpu
from jax.sharding import PartitionSpec as P

HEAD = 64
TILE = 8
TOKENS = TILE * TILE
LANES = 256
PER = LANES // HEAD
MARKS = 16
SCALE = HEAD ** -0.5
LOG2E = 1.4426950408889634
NEG = -1e30
BIG = 1e30
LIMIT = 20 * 1024 * 1024
VMEM = pl.BlockSpec(memory_space=pltpu.VMEM)
SMEM = pl.BlockSpec(memory_space=pltpu.SMEM)
BF16 = jnp.bfloat16
F32 = jnp.float32


def shift(array, axis, by):
    count = lax.axis_size(axis)
    pairs = [(i, i + by) for i in range(count) if 0 <= i + by < count]
    return lax.ppermute(array, axis, pairs)


def nt(a, b):
    return lax.dot_general(a, b, (((1,), (1,)), ((), ())), preferred_element_type=F32)


def nn(a, b):
    return lax.dot_general(a, b, (((1,), (0,)), ((), ())), preferred_element_type=F32)


def tn(a, b):
    return lax.dot_general(a, b, (((0,), (0,)), ((), ())), preferred_element_type=F32)


def call(body, out_shape, args, flops=0, exps=0):
    size = sum(array.size * array.dtype.itemsize for array in args)
    return pl.pallas_call(
        body,
        in_specs=[VMEM] * len(args),
        out_specs=[VMEM] * len(out_shape),
        out_shape=out_shape,
        compiler_params=pltpu.CompilerParams(vmem_limit_bytes=LIMIT),
        cost_estimate=pl.CostEstimate(flops=flops, transcendentals=exps, bytes_accessed=size),
    )(*args)


def tile_of(ref, a, b):
    block = ref[TILE * a : TILE * (a + 1), TILE * b : TILE * (b + 1), :]
    return block.astype(F32).reshape(TOKENS, block.shape[-1])


def put_tile(ref, a, b, lanes, value):
    shaped = value.reshape(TILE, TILE, value.shape[-1]).astype(ref.dtype)
    ref[TILE * a : TILE * (a + 1), TILE * b : TILE * (b + 1), lanes] = shaped


def rows_of(index):
    return slice(index * TOKENS, (index + 1) * TOKENS)


def mark_row(ref, start, index, lanes):
    return ref[start : start + MARKS, lanes].astype(F32)[index : index + 1]


def write_marks(out, start, marks, width):
    which = lax.broadcasted_iota(jnp.int32, (MARKS, width), 0)
    rows = jnp.zeros((MARKS, width), F32)
    for n, mark in enumerate(marks):
        rows = jnp.where(which == n, mark, rows)
    out[start : start + MARKS, :] = rows.astype(BF16)


def pack(grids, tissue, own_kv=None):
    rows, cols = tissue.shape
    width = grids[0].shape[-1]
    keys = own_kv is None

    def body(mark_hbm, *refs):
        sources, refs = refs[:2], refs[2:]
        kv_refs, refs = ((), refs) if keys else (refs[:rows], refs[rows:])
        row_refs, side_refs = refs[:rows], refs[rows : rows + (0 if keys else 2)]
        *grid_refs, sems, mark_ref, mark_sem = refs[-5:]
        copies = [
            [
                pltpu.make_async_copy(
                    source.at[TILE * a : TILE * (a + 1)], ref.at[TILE * a : TILE * (a + 1)], sems.at[n, a]
                )
                for a in range(rows)
            ]
            for n, (source, ref) in enumerate(zip(sources, grid_refs))
        ]
        for copy in sum(copies, []):
            copy.start()
        marks = pltpu.make_async_copy(mark_hbm, mark_ref, mark_sem)
        marks.start()
        marks.wait()
        for end, side in zip((0, cols - 1), side_refs):
            for n in range(2):
                for a in range(rows):
                    side[rows_of(n * rows + a), :] = kv_refs[a][rows_of(n * cols + end), :]
            write_marks(side, 4 * rows * TOKENS, [mark_ref[a, end].astype(F32) for a in range(rows)], width)
        for n, ref in enumerate(grid_refs):
            for a in range(rows):
                copies[n][a].wait()
                for b in range(cols):
                    tile = tile_of(ref, a, b)
                    if not keys:
                        tile = tile * (SCALE if n == 0 else mark_ref[a, b].astype(F32))
                    tile = tile.astype(BF16)
                    row_refs[a][rows_of(n * cols + b), :] = tile
                    for end, side in zip((0, cols - 1), side_refs):
                        if b == end:
                            side[rows_of((n + 2) * rows + a), :] = tile
        if keys:
            for a in range(rows):
                write_marks(row_refs[a], 2 * cols * TOKENS, [mark_ref[a, b].astype(F32) for b in range(cols)], width)

    heights = [2 * cols * TOKENS + (MARKS if keys else 0)] * rows + [4 * rows * TOKENS + MARKS] * (0 if keys else 2)
    shapes = [jax.ShapeDtypeStruct((height, width), BF16) for height in heights]
    return pl.pallas_call(
        body,
        in_specs=[pl.BlockSpec(memory_space=pltpu.HBM)] * 3 + [VMEM] * (0 if keys else rows),
        out_specs=[VMEM] * len(shapes),
        out_shape=shapes,
        scratch_shapes=[pltpu.VMEM(grid.shape, grid.dtype) for grid in grids] + [pltpu.SemaphoreType.DMA((2, rows))]
        + [pltpu.SMEM(tissue.shape, jnp.int32), pltpu.SemaphoreType.DMA],
        compiler_params=pltpu.CompilerParams(vmem_limit_bytes=LIMIT),
        cost_estimate=pl.CostEstimate(flops=0, transcendentals=0, bytes_accessed=1 << 20),
    )(*(pltpu.with_memory_space_constraint(array, pltpu.HBM) for array in (tissue, *grids)), *(own_kv or ()))


def pack_corners(above, below, cols):
    width = above.shape[1]

    def body(above_ref, below_ref, *outs):
        for b, out in zip((0, cols - 1), outs):
            for n in range(2):
                for end, ref in enumerate((above_ref, below_ref)):
                    out[rows_of(n * 2 + end), :] = ref[rows_of(n * cols + b), :]
            ends = [mark_row(ref, 2 * cols * TOKENS, b, slice(None)) for ref in (above_ref, below_ref)]
            write_marks(out, 4 * TOKENS, ends, width)

    shape = jax.ShapeDtypeStruct((4 * TOKENS + MARKS, width), BF16)
    return call(body, [shape] * 2, (above, below))


def pieces(x):
    out = []
    for _ in range(3):
        out.append(x.astype(BF16))
        x = x - out[-1].astype(F32)
    return out


def pack_queries(stats, above_s, below_s, above_qg, below_qg, cols):
    rows = len(stats)
    width = above_s.shape[1]
    height = -(-6 * (rows + 2) // MARKS) * MARKS

    def body(*refs):
        stat_refs, ends, outs = refs[: rows + 2], refs[rows + 2 : rows + 4], refs[rows + 4 :]
        for b, out in zip((0, cols - 1), outs):
            for n in range(2):
                for end, ref in enumerate(ends):
                    out[rows_of(n * 2 + end), :] = ref[rows_of(n * cols + b), :]
            parts = pieces(jnp.concatenate([ref[2 * b : 2 * b + 2, :] for ref in stat_refs], axis=0))
            parts = [part.astype(F32) for part in parts]
            rest = height - 6 * (rows + 2)
            if rest:
                parts.append(jnp.zeros((rest, width), F32))
            out[4 * TOKENS :, :] = jnp.concatenate(parts, axis=0).astype(BF16)

    shape = jax.ShapeDtypeStruct((4 * TOKENS + height, width), BF16)
    return call(body, [shape] * 2, (*stats, above_s, below_s, above_qg, below_qg))


def head_mask():
    row = lax.broadcasted_iota(jnp.int32, (LANES, LANES), 0) // HEAD
    lane = lax.broadcasted_iota(jnp.int32, (LANES, LANES), 1) // HEAD
    return row == lane


def spread(tile, mask):
    return jnp.where(mask, jnp.concatenate([tile] * PER, axis=0), jnp.zeros((), tile.dtype))


def gather_heads(full):
    lane = lax.broadcasted_iota(jnp.int32, (TOKENS, LANES), 1) // HEAD
    out = full[:TOKENS]
    for h in range(1, PER):
        out = jnp.where(lane == h, full[h * TOKENS : (h + 1) * TOKENS], out)
    return out


def fold(x, op):
    return op(x.reshape(x.shape[0] // 8, 8, x.shape[1]), axis=0)


class Block:
    def __init__(self, rows, cols, own, near, lanes):
        self.rows, self.cols, self.own, self.lanes = rows, cols, own, lanes
        self.above, self.below, self.left, self.right, self.corner_left, self.corner_right = near

    def tile(self, n, i, j, side):
        ends = {-1: (self.above, 0), self.rows: (self.below, 1)}
        if 0 <= j < self.cols:
            ref = ends[i][0] if i in ends else self.own[i]
            return ref[rows_of(n * self.cols + j), self.lanes]
        if i in ends:
            ref = self.corner_left if j < 0 else self.corner_right
            return ref[rows_of(n * 2 + ends[i][1]), self.lanes]
        ref = self.left if j < 0 else self.right
        return ref[rows_of((side + n) * self.rows + i), self.lanes]

    def mark(self, i, j):
        ends = {-1: (self.above, 0), self.rows: (self.below, 1)}
        if 0 <= j < self.cols:
            if i not in ends:
                return mark_row(self.own[i], 2 * self.cols * TOKENS, j, self.lanes)
            return mark_row(ends[i][0], 2 * self.cols * TOKENS, j, self.lanes)
        if i in ends:
            ref = self.corner_left if j < 0 else self.corner_right
            return mark_row(ref, 4 * TOKENS, ends[i][1], self.lanes)
        ref = self.left if j < 0 else self.right
        return mark_row(ref, 4 * self.rows * TOKENS, i, self.lanes)


WIDTH = 8


def drive(programs):
    active, waiting = [], list(programs)
    while active or waiting:
        active, waiting = active + waiting[:WIDTH], waiting[WIDTH:]
        active = [program for program in active if next(program, True) is None]


def around(a, b):
    return [(a + i, b + j) for j in (-1, 0, 1) for i in (-1, 0, 1)]


def each_group(width, programs):
    drive(sum((list(programs(pl.ds(g * LANES, LANES))) for g in range(width // LANES)), []))


def columns(first, second):
    rows = jnp.concatenate(
        [part.astype(F32) for row in (first, second) for part in pieces(row) + [jnp.zeros_like(row)] * 5], axis=0
    )
    index = lax.broadcasted_iota(jnp.int32, (MARKS, LANES), 0) // 8
    lane = lax.broadcasted_iota(jnp.int32, (MARKS, LANES), 1) // 128
    full = tn(rows.astype(BF16), jnp.where(index == lane, 1.0, 0.0).astype(BF16))
    return [
        gather_heads(jnp.concatenate([full[:, 128 * n : 128 * (n + 1)]] * (LANES // 128), axis=1)) for n in range(2)
    ]


def softmax_part(scores, allowed, top):
    for t, ok in enumerate(allowed):
        high = fold(scores[rows_of(t)], jnp.max)
        if ok is not None:
            high = jnp.where(ok, high, NEG)
        high = high * LOG2E
        top = high if top is None else jnp.maximum(top, high)
    return jnp.max(top, axis=0, keepdims=True)


def exponentials(scores, allowed, top):
    total = jnp.zeros((8, LANES), F32)
    low = []
    for t, ok in enumerate(allowed):
        less = top if ok is None else jnp.where(ok, top, BIG)
        e = jnp.exp2(scores[rows_of(t)] * LOG2E - less)
        total = total + fold(e, jnp.sum)
        low.append(e.astype(BF16))
    return jnp.concatenate(low, axis=0), jnp.sum(total, axis=0, keepdims=True)


def split_places(a, b, rows, cols):
    inside = [(i, j) for i, j in around(a, b) if 0 <= i < rows and 0 <= j < cols]
    return inside, [place for place in around(a, b) if place not in inside]


def forward_own(rows, cols, width):
    def body(*refs):
        own_kv, own_qg = refs[:rows], refs[rows : 2 * rows]
        part_ref, level_ref = refs[2 * rows :]
        mask = head_mask()

        def tile(block, lanes, a, b):
            places, _ = split_places(a, b, rows, cols)
            allowed = [None if place == (a, b) else block.mark(a, b) * block.mark(*place) > 0 for place in places]
            q = spread(own_qg[a][rows_of(b), lanes], mask)
            scores = nt(jnp.concatenate([block.tile(0, i, j, 0) for i, j in places], axis=0), q)
            yield
            top = softmax_part(scores, allowed, None)
            yield
            low, total = exponentials(scores, allowed, top)
            yield
            full = tn(low, jnp.concatenate([block.tile(1, i, j, 0) for i, j in places], axis=0))
            yield
            index = a * cols + b
            part_ref[rows_of(index), lanes] = gather_heads(full)
            level_ref[2 * index : 2 * index + 1, lanes] = top
            level_ref[2 * index + 1 : 2 * index + 2, lanes] = total

        def step(lanes):
            block = Block(rows, cols, own_kv, (None,) * 6, lanes)
            return (tile(block, lanes, a, b) for a in range(rows) for b in range(cols))

        each_group(width, step)

    return body


def corner_places(a, b, rows, cols):
    return [(i, j) for i, j in around(a, b) if not 0 <= i < rows and not 0 <= j < cols]


def place(a, b):
    return slice(TILE * a, TILE * (a + 1)), slice(TILE * b, TILE * (b + 1))


def finish(att_ref, a, b, lanes, att, grads):
    att = att.astype(BF16).astype(F32)
    put_tile(att_ref, a, b, lanes, att)
    prod = (grads.astype(F32) * att).T
    return jnp.concatenate([jnp.sum(prod[rows_of(h)], axis=0, keepdims=True) for h in range(PER)], axis=1)


def forward_near(rows, cols, width):
    def body(*refs):
        own_kv, near, own_qg = refs[:rows], refs[rows : rows + 4] + (None, None), refs[rows + 4 : 2 * rows + 4]
        part_ref, level_ref, part_out, level_out, att_ref = refs[2 * rows + 4 :]
        mask = head_mask()

        def tile(block, lanes, a, b):
            _, places = split_places(a, b, rows, cols)
            places = [place for place in places if place not in corner_places(a, b, rows, cols)]
            index = a * cols + b
            first = level_ref[2 * index : 2 * index + 1, lanes]
            before = level_ref[2 * index + 1 : 2 * index + 2, lanes]
            allowed = [block.mark(a, b) * block.mark(*place) > 0 for place in places]
            q = spread(own_qg[a][rows_of(b), lanes], mask)
            scores = nt(jnp.concatenate([block.tile(0, i, j, 0) for i, j in places], axis=0), q)
            yield
            top = softmax_part(scores, allowed, jnp.broadcast_to(first, (8, LANES)))
            yield
            low, total = exponentials(scores, allowed, top)
            less = jnp.exp2(first - top)
            yield
            full = tn(low, jnp.concatenate([block.tile(1, i, j, 0) for i, j in places], axis=0))
            total = total + less * before
            if corner_places(a, b, rows, cols):
                own_by, _ = columns(less, less)
                yield
                part_out[rows_of(index), lanes] = gather_heads(full) + part_ref[rows_of(index), lanes] * own_by
                level_out[2 * index : 2 * index + 1, lanes] = top
                level_out[2 * index + 1 : 2 * index + 2, lanes] = total
                return
            inverse = block.mark(a, b) / total
            near_by, own_by = columns(inverse, inverse * less)
            yield
            att = gather_heads(full) * near_by + part_ref[rows_of(index), lanes] * own_by
            dot = finish(att_ref, a, b, lanes, att, own_qg[a][rows_of(cols + b), lanes])
            level_out[2 * index : 2 * index + 1, lanes] = top + jnp.log2(total)
            level_out[2 * index + 1 : 2 * index + 2, lanes] = dot

        def step(lanes):
            block = Block(rows, cols, own_kv, near, lanes)
            return (tile(block, lanes, a, b) for a in range(rows) for b in range(cols))

        each_group(width, step)

    return body


def forward_last(rows, cols, width):
    def body(*refs):
        own_kv, refs = refs[:rows], refs[rows:]
        near, own_qg = (None,) * 4 + tuple(refs[:2]), refs[2 : rows + 2]
        part_ref, level_ref, att_ref, *stat_refs = refs[rows + 2 :]
        mask = head_mask()

        def tile(block, lanes, a, b):
            places = corner_places(a, b, rows, cols)
            index = a * cols + b
            own_mark = block.mark(a, b)
            if not places:
                stat_refs[a][2 * b : 2 * b + 2, lanes] = level_ref[2 * index : 2 * index + 2, lanes]
                return
            first = level_ref[2 * index : 2 * index + 1, lanes]
            before = level_ref[2 * index + 1 : 2 * index + 2, lanes]
            allowed = [own_mark * block.mark(*place) > 0 for place in places]
            q = spread(own_qg[a][rows_of(b), lanes], mask)
            scores = nt(jnp.concatenate([block.tile(0, i, j, 0) for i, j in places], axis=0), q)
            yield
            top = softmax_part(scores, allowed, jnp.broadcast_to(first, (8, LANES)))
            yield
            low, total = exponentials(scores, allowed, top)
            less = jnp.exp2(first - top)
            total = total + less * before
            full = tn(low, jnp.concatenate([block.tile(1, i, j, 0) for i, j in places], axis=0))
            inverse = own_mark / total
            near_by, own_by = columns(inverse, inverse * less)
            yield
            att = gather_heads(full) * near_by + part_ref[rows_of(index), lanes] * own_by
            dot = finish(att_ref, a, b, lanes, att, own_qg[a][rows_of(cols + b), lanes])
            stat_refs[a][2 * b : 2 * b + 1, lanes] = top + jnp.log2(total)
            stat_refs[a][2 * b + 1 : 2 * b + 2, lanes] = dot

        def step(lanes):
            block = Block(rows, cols, own_kv, near, lanes)
            return (tile(block, lanes, a, b) for a in range(rows) for b in range(cols))

        each_group(width, step)

    return body


def backward(rows, cols, width, tiles, kind):
    def body(*refs):
        count = 4 if kind == 0 else 6
        own_kv, near, refs = refs[:rows], (*refs[rows : rows + count], None, None)[:6], refs[rows + count :]
        own_qg, stat_refs, refs = refs[:rows], refs[rows : 2 * rows], refs[2 * rows :]
        moves = []
        if kind == 0:
            gq_ref, sum_ref = refs
            sum_ref[...] = jnp.zeros(sum_ref.shape, F32)
        elif kind == 1:
            _, middle_ref, edge_ref, att_ref, gq_ref, sum_ref, sems = refs
            for a in range(rows):
                for b in range(cols):
                    source = edge_ref if corner_places(a, b, rows, cols) else middle_ref
                    where = place(a, b)
                    moves.append(pltpu.make_async_copy(source.at[where], att_ref.at[where], sems.at[a * cols + b]))
                    moves[-1].start()
        else:
            _, gq_ref, sum_ref = refs
        mask = head_mask()

        def tile(block, lanes, a, b):
            places = around(a, b)
            own_mark = block.mark(a, b)
            q = spread(own_qg[a][rows_of(b), lanes], mask)
            g = spread(own_qg[a][rows_of(cols + b), lanes], mask)
            keys = jnp.concatenate([block.tile(0, i, j, 0) for i, j in places], axis=0)
            values = jnp.concatenate([block.tile(1, i, j, 0) for i, j in places], axis=0)
            index = a * cols + b if kind == 0 else b
            level = stat_refs[a][2 * index : 2 * index + 1, lanes]
            dot = stat_refs[a][2 * index + 1 : 2 * index + 2, lanes]
            scores, grads = nt(keys, q), nt(values, g)
            yield
            probs, slopes = [], []
            for t, spot in enumerate(places):
                less = level
                if spot != (a, b):
                    less = jnp.where(own_mark * block.mark(*spot) > 0, level, BIG)
                p = jnp.exp2(scores[rows_of(t)] * LOG2E - less)
                probs.append(p.astype(BF16))
                slopes.append((p * (grads[rows_of(t)] - dot)).astype(BF16))
            yield
            gq = gather_heads(tn(jnp.concatenate(slopes, axis=0), keys)) * SCALE
            put_tile(gq_ref, a, b, lanes, gq)
            inside = [t for t, (i, j) in enumerate(places) if 0 <= i < rows and 0 <= j < cols]
            for n, (parts, right) in enumerate(((slopes, q), (probs, g))):
                part = nn(jnp.concatenate([parts[t] for t in inside], axis=0), right)
                for u, t in enumerate(inside):
                    i, j = places[t]
                    sum_ref[n, rows_of(i * cols + j), lanes] += part[rows_of(u)]

        def step(lanes):
            block = Block(rows, cols, own_kv, near, lanes)
            return (tile(block, lanes, a, b) for a, b in tiles)

        each_group(width, step)
        for copy in moves:
            copy.wait()

    return body


def key_side(rows, cols, width, last):
    def body(*refs):
        own_kv, refs = refs[:rows], refs[rows:]
        if last:
            near_kv, near_qg, refs = (None, None, *refs[:4]), (None, None, *refs[4:8]), refs[8:]
            middle, gq_parts = refs[1:3], refs[3 : rows + 4]
            gq_ref, *out_refs, acc_ref, staged_k, staged_v, sems = refs[rows + 4 :]
            staged = (staged_k, staged_v)
            moves = []

            def move(source, target):
                moves.append(pltpu.make_async_copy(source, target, sems.at[len(moves)]))
                moves[-1].start()

            for a in range(rows):
                for b in range(cols):
                    where = place(a, b)
                    move(gq_parts[a + 1 if corner_places(a, b, rows, cols) else 0].at[where], gq_ref.at[where])
            if cols > 2:
                where = slice(None), slice(TILE, TILE * (cols - 1))
                for n in range(2):
                    move(middle[n].at[where], out_refs[n].at[where])
        else:
            near_kv, near_qg = (*refs[:2], *[None] * 4), (*refs[2:4], *[None] * 4)
            above_s, below_s, _, acc_ref, *staged = refs[4:]
        mask = head_mask()

        def stat_at(i, j, lanes):
            if 0 <= j < cols:
                ref = above_s if i < 0 else below_s
                return ref[2 * j : 2 * j + 1, lanes], ref[2 * j + 1 : 2 * j + 2, lanes]
            ref = near_qg[4 if j < 0 else 5]
            parts = ref[4 * TOKENS :, lanes].astype(F32)
            count = 2 * (rows + 2)
            stats = parts[:count] + parts[count : 2 * count] + parts[2 * count : 3 * count]
            n = rows if i < 0 else rows + 1 if i >= rows else i
            return stats[2 * n : 2 * n + 1], stats[2 * n + 1 : 2 * n + 2]

        def tile(marks, queries, lanes, i, j):
            places = [(x, y) for x, y in around(i, j) if 0 <= x < rows and 0 <= y < cols]
            q = spread(queries.tile(0, i, j, 2), mask)
            g = spread(queries.tile(1, i, j, 2), mask)
            level, dot = stat_at(i, j, lanes)
            mark = marks.mark(i, j)
            keys = jnp.concatenate([marks.tile(0, x, y, 0) for x, y in places], axis=0)
            values = jnp.concatenate([marks.tile(1, x, y, 0) for x, y in places], axis=0)
            scores, grads = nt(keys, q), nt(values, g)
            yield
            probs, slopes = [], []
            for t, (x, y) in enumerate(places):
                less = jnp.where(mark * marks.mark(x, y) > 0, level, BIG)
                p = jnp.exp2(scores[rows_of(t)] * LOG2E - less)
                probs.append(p.astype(BF16))
                slopes.append((p * (grads[rows_of(t)] - dot)).astype(BF16))
            yield
            for n, (parts, right) in enumerate(((slopes, q), (probs, g))):
                part = nn(jnp.concatenate(parts, axis=0), right)
                for t, (x, y) in enumerate(places):
                    acc_ref[n, rows_of(x * cols + y), lanes] += part[rows_of(t)]

        def step(lanes):
            marks = Block(rows, cols, own_kv, near_kv, lanes)
            queries = Block(rows, cols, None, near_qg, lanes)
            outside = [
                (i, j) for i in range(-1, rows + 1) for j in range(-1, cols + 1)
                if (not 0 <= j < cols if last else 0 <= j < cols and not 0 <= i < rows)
            ]
            return (tile(marks, queries, lanes, i, j) for i, j in outside)

        each_group(width, step)
        done = (0, cols - 1) if last else range(1, cols - 1)
        done = sorted(set(done))
        for g in range(width // LANES):
            lanes = pl.ds(g * LANES, LANES)
            for n in range(2):
                for y in done:
                    for x in range(rows):
                        put_tile(staged[n], x, y, lanes, acc_ref[n, rows_of(x * cols + y), lanes])
                    if last:
                        where = slice(None), slice(TILE * y, TILE * (y + 1)), lanes
                        move(staged[n].at[where], out_refs[n].at[where])
        if not last:
            return
        for copy in moves:
            copy.wait()

    return body


def local(query_grid, key_grid, value_grid, out_grad, tissue):
    rows, cols = tissue.shape
    width = query_grid.shape[-1]
    own_kv = pack((key_grid, value_grid), tissue)
    *own_qg, first_side, last_side = pack((query_grid, out_grad), tissue, own_kv)
    above_kv = shift(own_kv[-1], "rows", 1)
    below_kv = shift(own_kv[0], "rows", -1)
    grid_out = jax.ShapeDtypeStruct(query_grid.shape, BF16)
    stat_out = jax.ShapeDtypeStruct((2 * cols, width), F32)
    sum_out = jax.ShapeDtypeStruct((2, rows * cols * TOKENS, width), F32)
    part_out = jax.ShapeDtypeStruct((rows * cols * TOKENS, width), F32)
    level_out = jax.ShapeDtypeStruct((2 * rows * cols, width), F32)
    pairs = 9 * rows * cols * TOKENS * TOKENS * width
    part, level = call(
        forward_own(rows, cols, width), [part_out, level_out], (*own_kv, *own_qg),
        flops=64 * pairs, exps=pairs // HEAD * 8,
    )
    *sent_qg, level = lax.optimization_barrier((own_qg[0], own_qg[-1], level))
    left = shift(last_side, "cols", 1)
    right = shift(first_side, "cols", -1)
    above_qg = shift(sent_qg[1], "rows", 1)
    below_qg = shift(sent_qg[0], "rows", -1)
    above_kv, below_kv, level = lax.optimization_barrier((above_kv, below_kv, level))
    first_kv, last_kv = pack_corners(above_kv, below_kv, cols)
    part, level, middle = call(
        forward_near(rows, cols, width), [part_out, level_out, grid_out],
        (*own_kv, above_kv, below_kv, left, right, *own_qg, part, level), flops=64 * pairs, exps=pairs // HEAD * 8,
    )
    every = [(a, b) for a in range(rows) for b in range(cols)]
    hbm = pl.BlockSpec(memory_space=pltpu.HBM)

    def run(body, args, hbm_outs, vmem_outs, scratch, sums_at, sums_out, cost):
        return pl.pallas_call(
            body,
            in_specs=[VMEM] * len(args),
            out_specs=[hbm] * len(hbm_outs) + [VMEM] * len(vmem_outs),
            out_shape=hbm_outs + vmem_outs,
            scratch_shapes=scratch,
            input_output_aliases={} if sums_at is None else {sums_at: sums_out},
            compiler_params=pltpu.CompilerParams(vmem_limit_bytes=LIMIT),
            cost_estimate=pl.CostEstimate(flops=cost * pairs, transcendentals=cost * pairs // 32 // HEAD, bytes_accessed=1 << 20),
        )(*args)

    parts = []
    tiles = [spot for spot in every if not corner_places(*spot, rows, cols)]
    args = (*own_kv, above_kv, below_kv, left, right, *own_qg, *[level] * rows)
    part_gq, sums = run(backward(rows, cols, width, tiles, 0), args, [], [grid_out, sum_out], [], None, 1, 8)
    parts.append(part_gq)
    level, sums = lax.optimization_barrier((level, sums))
    corners_kv = (shift(last_kv, "cols", 1), shift(first_kv, "cols", -1))
    near_kv = (above_kv, below_kv, left, right, *corners_kv)
    edge, *stats = call(
        forward_last(rows, cols, width), [grid_out] + [stat_out] * rows,
        (*own_kv, *corners_kv, *own_qg, part, level), flops=4 * pairs, exps=pairs // (4 * HEAD),
    )
    above_s = shift(stats[-1], "rows", 1)
    below_s = shift(stats[0], "rows", -1)
    for a in range(rows):
        tiles = [spot for spot in every if spot[0] == a and corner_places(*spot, rows, cols)]
        args = (*own_kv, *near_kv, *own_qg, *stats, sums) + ((middle, edge) if a == 0 else ())
        *done, part_gq, sums = run(
            backward(rows, cols, width, tiles, 1 if a == 0 else 2), args, [grid_out] * (a == 0), [grid_out, sum_out],
            [pltpu.SemaphoreType.DMA((rows * cols,))] * (a == 0), 3 * rows + 6, 2 if a == 0 else 1, 16,
        )
        parts.append(part_gq)
        if a == 0:
            attended = done[0]
            above_s, below_s, sums = lax.optimization_barrier((above_s, below_s, sums))
            first_q, last_q = pack_queries(stats, above_s, below_s, above_qg, below_qg, cols)
            side_qg = (left, right, shift(last_q, "cols", 1), shift(first_q, "cols", -1))
    args = (*own_kv, above_kv, below_kv, above_qg, below_qg, above_s, below_s, sums)
    sums, *inner = run(key_side(rows, cols, width, False), args, [], [sum_out, grid_out, grid_out], [], rows + 6, 0, 8)
    args = (*own_kv, *near_kv[2:], *side_qg, sums, *inner, *parts)
    grad_query, grad_key, grad_value, _ = run(
        key_side(rows, cols, width, True), args, [grid_out] * 3, [sum_out],
        [pltpu.VMEM(grid_out.shape, BF16)] * 2 + [pltpu.SemaphoreType.DMA((rows * cols + 2 + 4 * (width // LANES),))],
        rows + 8, 3, 8,
    )
    return attended, grad_query, grad_key, grad_value


def solution(mesh):
    grid = P(("groups", "rows"), "cols", None)
    return jax.shard_map(
        local,
        mesh=mesh,
        in_specs=(grid, grid, grid, grid, P(("groups", "rows"), "cols")),
        out_specs=(grid, grid, grid, grid),
        check_vma=False,
    )
```
